32 devices in a mesh: grp: 2 (over x), gx: 8 (over z, y), gy: 2 (over core).
Axes of the slice: x: 2, y: 2, z: 4, core: 2. Of those that a mesh axis runs over, the one named last changes fastest.
Arguments:
- spectrum: float32 [16, 96, 1152], P('gx', 'gy', 'grp'), may hold values from 0 to 2
- wet_mask: int32 [16, 96], P('gx', 'gy'), may hold values 0 or 1
- ocean_source: int32 [16, 96], P('gx', 'gy'), may hold values from 0 to 95
- ocean_u: float32 [16, 96, 40], P('gx', 'gy', 'grp'), may hold values from -2 to 2
- ocean_v: float32 [16, 96, 40], P('gx', 'gy', 'grp'), may hold values from -2 to 2
- current_weights: float32 [40, 32], replicated, may hold values from 0.005 to 0.04
- drift_weights: float32 [40, 32], replicated, may hold values from 0.005 to 0.05
- inter_left: bfloat16 [1152, 512], P('grp'), may hold values from -0.25 to 0.25
- inter_right: bfloat16 [1152, 512], P('grp'), may hold values from -0.25 to 0.25
- inter_out: bfloat16 [512, 1152], P(None, 'grp'), may hold values from -0.25 to 0.25
- mixing: float32 [40, 40], P(None, 'grp'), may hold values from -0.47434166 to 0.47434166
Outputs:
- spectrum_out: float32 [16, 96, 1152], P('gx', 'gy', 'grp')
- ocean_u_out: float32 [16, 96, 40], P('gx', 'gy', 'grp')
- ocean_v_out: float32 [16, 96, 40], P('gx', 'gy', 'grp')
- drift_u: float32 [16, 96, 40], P('gx', 'gy', 'grp')
- drift_v: float32 [16, 96, 40], P('gx', 'gy', 'grp')
The draws below stay inside these ranges and needn't reach their ends.
Inputs may be any that keep to these rules, and one draw needn't show every extreme that they name: `wet_mask`: 1 marks a sea column, 0 a land column. `ocean_source`: each entry numbers a column of the same tile of 2 x 48 columns as (x mod 2) * 48 + (y mod 48).
All inputs are finite; a program needn't handle non-finite values. No bound on the sum of `wet_mask` on one device may be relied on, other than what follows from the above.
Results may differ from the reference program's by a relative error of at most 0.00077.
Values sent between devices are 32-bit elements; how exact they have to be, the bound alone decides.
A program may use at most 64 MiB of HBM per device.

```python
import math
import jax
import jax.numpy as jnp
from jax import lax

NF = 32
ND = 36
NLEV = 40
RANK = 512
WAVE_SECTIONS = 3
OCEAN_SECTIONS = 2
CX = 2
CY = 48
NX = 16
NY = 96
NBIN = 1152
NFL = 16


def touch_ends(result, stream_key, smallest, high):
    index_at = [jax.random.randint(jax.random.fold_in(stream_key, axis), (), 0, length) for axis, length in enumerate(result.shape)]
    main_axis = result.shape.index(max(result.shape))
    beside = index_at[:main_axis] + [(index_at[main_axis] + 1) % result.shape[main_axis]] + index_at[main_axis + 1:]
    return result.at[tuple(index_at)].set(smallest).at[tuple(beside)].set(high)


def block_scale(own_key, shape, pieces, low, largest):
    level, own = 1.0, jax.random.fold_in(own_key, 6)
    for dim, shards_of in pieces:
        steps = jnp.exp(jax.random.uniform(jax.random.fold_in(own, dim), (shards_of,), jnp.float32, low / len(pieces), largest / len(pieces)))
        level = level * jnp.repeat(steps, shape[dim] // shards_of).reshape([-1 if axis == dim else 1 for axis in range(len(shape))])
    return level


def noise(own_key, dims, spread, most, pieces=(), dtype=jnp.bfloat16):
    gain = block_scale(own_key, dims, pieces, -0.22, 0.18) if pieces else 1.0
    array = jax.random.normal(own_key, dims, jnp.float32) * spread * gain
    return jnp.minimum(jnp.maximum(array, -most), most).astype(dtype)


def setup_inputs(seed: int = 0) -> dict:
    splits = jax.random.split(jax.random.key(seed), 12)
    return {
        "spectrum": jnp.clip(2.0 * jax.random.uniform(splits[0], (NX, NY, NBIN), jnp.float32) ** block_scale(splits[0], (NX, NY, NBIN), ((0, 8), (1, 2), (2, 2)), -0.2, 0.2), 0.0, 2.0),
        "wet_mask": touch_ends((jax.random.randint(splits[1], (NX, NY), 0, 5) < 4).astype(jnp.int32), jax.random.fold_in(splits[1], 1), 0, 1),
        "ocean_source": touch_ends(jax.random.randint(splits[2], (NX, NY), 0, CX * CY), jax.random.fold_in(splits[2], 1), 0, (CX * CY) - 1).astype(jnp.int32),
        "ocean_u": noise(splits[3], (NX, NY, NLEV), 0.5, 2.0, ((0, 8), (1, 2), (2, 2)), jnp.float32),
        "ocean_v": noise(splits[4], (NX, NY, NLEV), 0.5, 2.0, ((0, 8), (1, 2), (2, 2)), jnp.float32),
        "current_weights": jnp.clip(jnp.exp(jax.random.uniform(splits[5], (NLEV, NF), jnp.float32, math.log(0.005), math.log(0.04))), 0.005, 0.04),
        "drift_weights": jnp.clip(jnp.exp(jax.random.uniform(splits[6], (NLEV, NF), jnp.float32, math.log(0.005), math.log(0.05))), 0.005, 0.05),
        "inter_left": noise(splits[7], (NBIN, RANK), (NBIN // 2) ** -0.5, 0.25, ((0, 2),)),
        "inter_right": noise(splits[8], (NBIN, RANK), (NBIN // 2) ** -0.5, 0.25, ((0, 2),)),
        "inter_out": noise(splits[9], (RANK, NBIN), RANK ** -0.5, 0.25, ((1, 2),)),
        "mixing": noise(splits[10], (NLEV, NLEV), (0.5 / NLEV ** 0.5), 0.47434166, ((1, 2),), jnp.float32),
    }


highest = lax.Precision.HIGHEST
inter_step = 0.1
ocean_step = 0.4
coriolis = 0.5
viscosity = 0.1


def bin_tables(band_index, bin_count):
    position = jnp.arange(bin_count)
    direction = (position // NFL).astype(jnp.float32)
    frequency = (band_index * NFL + position % NFL).astype(jnp.float32)
    angle_value = 2.0 * jnp.pi * direction / ND
    group_speed = 0.2 + 0.4 * (NF - 1 - frequency) / (NF - 1)
    turning = 0.5 * (frequency + 1.0) / NF
    return jnp.cos(angle_value), jnp.sin(angle_value), group_speed, turning


def beam_sweep(padded, velocity, which_axis):
    extent = velocity.shape[which_axis]

    def take_part(offset):
        return lax.slice_in_dim(padded, offset, offset + extent, axis=which_axis)

    centre = take_part(2)
    upwind_one = jnp.where(velocity >= 0.0, take_part(1), take_part(3))
    beyond = jnp.where(velocity >= 0.0, take_part(0), take_part(4))
    magnitude = jnp.abs(velocity)
    return centre - 0.5 * magnitude * (3.0 * centre - 4.0 * upwind_one + beyond) + 0.5 * magnitude * magnitude * (centre - 2.0 * upwind_one + beyond)


def wave_section(spectrum_now, speed_x, speed_y, turn_rate, left_band, right_band, out_band, wet_factor):
    padded = jnp.pad(spectrum_now, ((2, 2), (0, 0), (0, 0)))
    shifted = beam_sweep(padded, speed_x, 0)
    padded = jnp.pad(shifted, ((0, 0), (2, 2), (0, 0)))
    shifted = beam_sweep(padded, speed_y, 1)
    behind = jnp.roll(shifted, NFL, axis=2)
    ahead_dir = jnp.roll(shifted, -NFL, axis=2)
    upwind = jnp.where(turn_rate >= 0.0, behind, ahead_dir)
    turned = shifted - jnp.abs(turn_rate) * (shifted - upwind)
    flat_bins = spectrum_now.reshape(-1, spectrum_now.shape[2]).astype(jnp.bfloat16)
    product = jnp.dot(flat_bins, left_band, preferred_element_type=jnp.float32) * jnp.dot(flat_bins, right_band, preferred_element_type=jnp.float32)
    source = inter_step * jnp.dot(product.astype(jnp.bfloat16), out_band, preferred_element_type=jnp.float32)
    return wet_factor * (turned + source.reshape(spectrum_now.shape))


def laplace(values):
    padded = jnp.pad(values, ((1, 1), (1, 1), (0, 0)))
    return padded[2:, 1:-1] + padded[:-2, 1:-1] + padded[1:-1, 2:] + padded[1:-1, :-2] - 4.0 * values


def reference(spectrum, wet_mask, ocean_source, ocean_u, ocean_v, current_weights, drift_weights, inter_left, inter_right, inter_out, mixing):
    wet_factor = wet_mask.astype(jnp.float32)[:, :, None]
    columns_x = jnp.arange(NX)[:, None]
    columns_y = jnp.arange(NY)[None, :]
    source_x = (columns_x // CX) * CX + ocean_source // CY
    source_y = (columns_y // CY) * CY + ocean_source % CY
    source_u = ocean_u[source_x, source_y]
    source_v = ocean_v[source_x, source_y]
    bin_count = NBIN // 2
    kept_bands = []
    drift_x = jnp.zeros((NX, NY, NLEV), jnp.float32)
    drift_y = jnp.zeros((NX, NY, NLEV), jnp.float32)
    for band_index in range(2):
        cosine, sine_value, group_speed, turning = bin_tables(band_index, bin_count)
        weights_band = current_weights[:, band_index * NFL:(band_index + 1) * NFL]
        flow_x = jnp.tile(jnp.einsum("abk,kf->abf", source_u, weights_band, precision=highest), (1, 1, ND))
        flow_y = jnp.tile(jnp.einsum("abk,kf->abf", source_v, weights_band, precision=highest), (1, 1, ND))
        speed_x = group_speed * cosine + flow_x
        speed_y = group_speed * sine_value + flow_y
        turn_rate = turning * (sine_value * flow_x - cosine * flow_y)
        lower = band_index * bin_count
        upper = lower + bin_count
        spectrum_now = wet_factor * spectrum[:, :, lower:upper]
        for repeat in range(WAVE_SECTIONS):
            spectrum_now = wave_section(spectrum_now, speed_x, speed_y, turn_rate, inter_left[lower:upper], inter_right[lower:upper], inter_out[:, lower:upper], wet_factor)
        kept_bands.append(spectrum_now)
        profile = jnp.tile(drift_weights[:, band_index * NFL:(band_index + 1) * NFL], (1, ND))
        drift_x = drift_x + jnp.einsum("abn,kn->abk", spectrum_now, profile * cosine, precision=highest)
        drift_y = drift_y + jnp.einsum("abn,kn->abk", spectrum_now, profile * sine_value, precision=highest)
    spectrum_out = jnp.concatenate(kept_bands, axis=2)
    velocity_u = ocean_u
    velocity_v = ocean_v
    for repeat in range(OCEAN_SECTIONS):
        first_u = velocity_u + ocean_step * (coriolis * (velocity_v + drift_y) + viscosity * laplace(velocity_u))
        first_v = velocity_v + ocean_step * (-coriolis * (velocity_u + drift_x) + viscosity * laplace(velocity_v))
        velocity_u = wet_factor * (first_u + jnp.einsum("abk,kl->abl", first_u, mixing, precision=highest))
        velocity_v = wet_factor * (first_v + jnp.einsum("abk,kl->abl", first_v, mixing, precision=highest))
    return spectrum_out, velocity_u, velocity_v, drift_x, drift_y
```

```python
import functools

import jax
import jax.numpy as jnp
import numpy as np
from jax import lax
from jax.experimental import pallas as pl
from jax.experimental.pallas import tpu as pltpu
from jax.sharding import PartitionSpec as P

NF = 32
ND = 36
NLEV = 40
WAVE_SECTIONS = 3
NFL = 16
LANES = 128
MESH = pl.DeviceIdType.MESH

highest = lax.Precision.HIGHEST
inter_step = 0.1
ocean_step = 0.4
coriolis = 0.5
viscosity = 0.1


def exact_dot(a, b):
    return jnp.dot(a, b, precision=highest, preferred_element_type=jnp.float32)


def sweep(centre, back_one, back_two, next_one, next_two, velocity):
    up = velocity >= 0.0
    one = jnp.where(up, back_one, next_one)
    two = jnp.where(up, back_two, next_two)
    size = jnp.abs(velocity)
    half = 0.5 * size
    return centre - half * (3.0 * centre - 4.0 * one + two) + half * size * (centre - 2.0 * one + two)


def iota(shape, dim):
    return lax.broadcasted_iota(jnp.int32, shape, dim)


class Move:
    def __init__(self, src, dst, send, recv, device, sends, receives):
        self.copy = pltpu.make_async_remote_copy(
            src_ref=src, dst_ref=dst, send_sem=send, recv_sem=recv, device_id=device, device_id_type=MESH
        )
        self.sends, self.receives = sends, receives

    def when(self, cond, act):
        if cond is True:
            act()
        else:
            pl.when(cond)(act)

    def start(self):
        self.when(self.sends, self.copy.start)

    def wait_send(self):
        self.when(self.sends, self.copy.wait_send)

    def wait_recv(self):
        self.when(self.receives, self.copy.wait_recv)


def kernel(
    sizes,
    spectrum,
    pack,
    angles,
    cw,
    dw,
    left,
    right,
    out_map,
    spec_out,
    u_out,
    v_out,
    du_out,
    dv_out,
    masked,
    packs,
    own_flow,
    flow,
    flow_edge,
    flow_halo,
    field,
    edge,
    halo_x,
    halo_y,
    speed_x,
    speed_y,
    turn,
    speed_l,
    speed_r,
    wide,
    source,
    mix,
    ocean,
    ocean_next,
    row_halo,
    col_edge,
    col_halo,
    drift_q,
    drift_n,
    init_send,
    init_recv,
    wave_send,
    wave_recv,
    sea_send,
    sea_recv,
):
    nx, ny = sizes
    tile_x, tile_y, bins = spectrum.shape
    half = tile_y // 2
    own = u_out.shape[2]
    rows = 2 * tile_x
    g, gx, gy = lax.axis_index("grp"), lax.axis_index("gx"), lax.axis_index("gy")
    z, y = gx // 2, gx % 2
    q = 2 * gy + y
    nz, nq = nx // 2, 2 * ny

    def at(dg=0, x=gx, c=gy):
        return {"grp": (g + dg) % 2, "gx": x, "gy": c}

    pair = 2 * z + 1 - y

    def q_at(dz, dq):
        qq = q + dq
        return at(0, 2 * (z + dz) + qq % 2, qq // 2)

    def inside(value, step, limit):
        return value + step >= 0 if step < 0 else value + step < limit

    def both(dz, dq):
        cond = inside(q, dq, nq)
        return cond if dz == 0 else cond & inside(z, dz, nz)

    friends = [(True, at(1)), (True, at(0, pair)), (True, at(1, pair))]
    friends += [(inside(z, d, nz), at(0, gx + 2 * d)) for d in (-1, 1)]
    friends += [(both(dz, dq), q_at(dz, dq)) for dq in (-1, 1) for dz in (-1, 0, 1)]
    friends += [(inside(gx, d, nx), at(0, gx + d)) for d in (-1, 1)]
    friends += [(inside(gy, d, ny), at(0, gx, gy + d)) for d in (-1, 1)]
    barrier = pltpu.get_barrier_semaphore()
    total = 0
    for cond, device in friends:

        def hello(device=device):
            pl.semaphore_signal(barrier, inc=1, device_id=device, device_id_type=MESH)

        if cond is True:
            hello()
            total = total + 1
        else:
            pl.when(cond)(hello)
            total = total + jnp.where(cond, 1, 0)

    columns = tile_x * tile_y
    wet_n = pack[0:columns, 2 * own : 2 * own + 1]
    masked[...] = (spectrum[...].reshape(columns, bins) * wet_n).reshape(tile_x, tile_y, bins)

    @pl.when(z == 0)
    def _():
        halo_x[:, 0] = jnp.zeros_like(halo_x[:, 0])

    @pl.when(z == nz - 1)
    def _():
        halo_x[:, 1] = jnp.zeros_like(halo_x[:, 1])

    for side, dq in ((0, -1), (1, 1)):

        @pl.when(jnp.logical_not(inside(q, dq, nq)))
        def _():
            halo_y[:, side] = jnp.zeros_like(halo_y[:, side])
            flow_halo[side] = jnp.zeros_like(flow_halo[side])

        for slot, dz in ((0, -1), (2, 1)):

            @pl.when(inside(q, dq, nq) & jnp.logical_not(inside(z, dz, nz)))
            def _():
                halo_y[:, side, slot] = jnp.zeros_like(halo_y[:, side, slot])

    for side, d in ((0, -1), (1, 1)):

        @pl.when(jnp.logical_not(inside(gx, d, nx)))
        def _():
            row_halo[:, side] = jnp.zeros_like(row_halo[:, side])

        @pl.when(jnp.logical_not(inside(gy, d, ny)))
        def _():
            col_halo[:, side] = jnp.zeros_like(col_halo[:, side])

    pl.semaphore_wait(barrier, total)

    to_grp = Move(pack, packs, init_send.at[0], init_recv.at[0], at(1), True, True)
    to_grp.start()
    away = pl.ds(pl.multiple_of(half * (1 - y), 8), half)
    mine = pl.ds(pl.multiple_of(half * y, 8), half)
    my_rows = pl.ds(tile_x * y, tile_x)
    to_pair = Move(
        masked.at[:, away, :], field.at[my_rows], init_send.at[1], init_recv.at[1], at(0, pair), True, True
    )
    to_pair.start()
    field[my_rows] = masked[:, mine, :]

    place_i, place_j = iota((LANES, LANES), 0), iota((LANES, LANES), 1)

    def placing(group):
        shift = own * group + jnp.where(place_i < own, 0, own)
        keep = (place_i < 2 * own) & (place_j == place_i + shift)
        return jnp.where(keep, 1.0, 0.0)

    to_grp.wait_recv()
    everything = exact_dot(pack[...], placing(g)) + exact_dot(packs[...], placing(1 - g))
    ocean[...] = everything[:columns].reshape(ocean.shape)
    mix[...] = jnp.zeros_like(mix)
    mix[0:NLEV] = everything[columns:]
    mix[NLEV : 2 * NLEV] = pltpu.roll(everything[columns:], NLEV, 1)
    chosen = jnp.where(iota((columns, columns), 1).astype(jnp.float32) == pack[0:columns, 2 * own + 1 : 2 * own + 2], 1.0, 0.0)
    felt = exact_dot(chosen, exact_dot(everything[:columns], cw[...]))
    felt = felt + jnp.where(iota((columns, LANES), 1) == 2 * NF, wet_n, 0.0)
    own_flow[...] = felt.reshape(own_flow.shape)
    flow_pair = Move(
        own_flow.at[:, away, :], flow.at[my_rows], init_send.at[2], init_recv.at[2], at(0, pair), True, True
    )
    flow_pair.start()
    flow[my_rows] = own_flow[:, mine, :]

    def sea_moves(k, array):
        moves = []
        for side, d in ((0, -1), (1, 1)):
            moves.append(
                Move(
                    array.at[0 if d < 0 else tile_x - 1],
                    row_halo.at[k, 1 - side],
                    sea_send.at[k, side],
                    sea_recv.at[k, side],
                    at(0, gx + d),
                    inside(gx, d, nx),
                    inside(gx, -d, nx),
                )
            )
            moves.append(
                Move(
                    col_edge.at[k, side],
                    col_halo.at[k, 1 - side],
                    sea_send.at[k, 2 + side],
                    sea_recv.at[k, 2 + side],
                    at(0, gx, gy + d),
                    inside(gy, d, ny),
                    inside(gy, -d, ny),
                )
            )
        return moves

    def set_col_edges(k, array):
        for side, column in ((0, 0), (1, tile_y - 1)):
            for r in range(tile_x):
                col_edge[k, side, r : r + 1, :] = array[r, column : column + 1, :]

    lane = iota((1, bins), 1)
    frequency = (g * NFL + (lane & (NFL - 1))).astype(jnp.float32)
    group_speed = 0.2 + 0.4 * (NF - 1 - frequency) / (NF - 1)
    turning = 0.5 * (frequency + 1.0) / NF
    cosine, sine = angles[0:1, :], angles[1:2, :]
    spread_i = iota((LANES, bins), 0)
    spread_f = g * NFL + (iota((LANES, bins), 1) & (NFL - 1))
    spread_x = jnp.where(spread_i == spread_f, 1.0, 0.0)
    spread_y = jnp.where(spread_i == spread_f + NF, 1.0, 0.0)

    def wave_moves(s):
        moves = []
        for side, dz in ((0, -1), (1, 1)):
            moves.append(
                Move(
                    field.at[pl.ds(0 if dz < 0 else rows - 2, 2)],
                    halo_x.at[s, 1 - side],
                    wave_send.at[s, side],
                    wave_recv.at[s, side],
                    at(0, gx + 2 * dz),
                    inside(z, dz, nz),
                    inside(z, -dz, nz),
                )
            )
        k = 2
        for side, dq in ((0, -1), (1, 1)):
            for dz in (-1, 0, 1):
                moves.append(
                    Move(
                        edge.at[s, side],
                        halo_y.at[s, 1 - side, 1 - dz],
                        wave_send.at[s, k],
                        wave_recv.at[s, k],
                        q_at(dz, dq),
                        both(dz, dq),
                        both(-dz, -dq),
                    )
                )
                k += 1
        return moves

    def set_edges(s):
        for side, first in ((0, 0), (1, half - 2)):
            for r in range(rows):
                edge[s, side, 2 * r : 2 * r + 2, :] = field[r, first : first + 2, :]

    def interaction():
        now = field[...].reshape(rows * half, bins).astype(jnp.bfloat16)
        product = jnp.dot(now, left[...], preferred_element_type=jnp.float32) * jnp.dot(
            now, right[...], preferred_element_type=jnp.float32
        )
        result = jnp.dot(product.astype(jnp.bfloat16), out_map[...], preferred_element_type=jnp.float32)
        source[...] = (inter_step * result).reshape(source.shape)

    def finish(s, moves):
        for m in moves:
            m.wait_recv()
        for side, speed, start in ((0, speed_l, 6), (1, speed_r, half + 8)):
            before, here, after = (halo_y[s, side, i] for i in range(3))
            low = iota((8, bins), 0)

            def joined(a, b, n):
                return jnp.where(low < n, pltpu.roll(a, n, 0), pltpu.roll(b, n, 0))

            packed = sweep(
                here,
                joined(before, here, 2),
                joined(before, here, 4),
                joined(here, after, 6),
                joined(here, after, 4),
                speed[...],
            )
            for r in range(rows):
                wide[r, start : start + 2, :] = packed[2 * r : 2 * r + 2]

        def line(r):
            if r < 0:
                return halo_x[s, 0, r + 2]
            if r >= rows:
                return halo_x[s, 1, r - rows]
            return field[r]

        for r in range(rows):
            wide[r, 8 : 8 + half, :] = sweep(
                line(r), line(r - 1), line(r - 2), line(r + 1), line(r + 2), speed_x[r]
            )
        for m in moves:
            m.wait_send()
        for r in range(rows):
            b = sweep(
                wide[r, 8 : 8 + half, :],
                wide[r, 7 : 7 + half, :],
                wide[r, 6 : 6 + half, :],
                wide[r, 9 : 9 + half, :],
                wide[r, 10 : 10 + half, :],
                speed_y[r],
            )
            t = turn[r]
            behind = jnp.concatenate([b[:, bins - NFL :], b[:, : bins - NFL]], axis=1)
            ahead = jnp.concatenate([b[:, NFL:], b[:, :NFL]], axis=1)
            c = b - jnp.abs(t) * (b - jnp.where(t >= 0.0, behind, ahead))
            field[r] = flow[r, :, 2 * NF : 2 * NF + 1] * (c + source[r])

    def flow_moves():
        return [
            Move(
                flow_edge.at[side],
                flow_halo.at[1 - side],
                init_send.at[3 + side],
                init_recv.at[3 + side],
                q_at(0, dq),
                inside(q, dq, nq),
                inside(q, -dq, nq),
            )
            for side, dq in ((0, -1), (1, 1))
        ]

    to_pair.wait_recv()
    set_edges(0)
    first_moves = wave_moves(0)
    for m in first_moves:
        m.start()
    set_col_edges(0, ocean)
    flow_pair.wait_recv()
    for side, first in ((0, 0), (1, half - 2)):
        for r in range(rows):
            flow_edge[side, 2 * r : 2 * r + 2, :] = flow[r, first : first + 2, :]
    edges_flow = flow_moves()
    for m in edges_flow:
        m.start()
    sea_first = sea_moves(0, ocean)
    for m in sea_first:
        m.start()
    fq = flow[...].reshape(rows * half, LANES)
    fx = exact_dot(fq, spread_x)
    fy = exact_dot(fq, spread_y)
    speed_x[...] = (group_speed * cosine + fx).reshape(speed_x.shape)
    speed_y[...] = (group_speed * sine + fy).reshape(speed_x.shape)
    turn[...] = (turning * (sine * fx - cosine * fy)).reshape(speed_x.shape)
    interaction()
    for m in edges_flow:
        m.wait_recv()
    speed_l[...] = group_speed * cosine + exact_dot(flow_halo[0], spread_x)
    speed_r[...] = group_speed * cosine + exact_dot(flow_halo[1], spread_x)
    finish(0, first_moves)

    def section(s, carry):
        set_edges(s)
        moves = wave_moves(s)
        for m in moves:
            m.start()
        interaction()
        finish(s, moves)
        return carry

    lax.fori_loop(1, WAVE_SECTIONS, section, 0)

    their_rows = pl.ds(tile_x * (1 - y), tile_x)
    back = Move(
        field.at[their_rows], spec_out.at[:, mine, :], init_send.at[5], init_recv.at[5], at(0, pair), True, True
    )
    depth = exact_dot(dw[...], spread_x)
    unused = jnp.zeros((LANES - 2 * NLEV, bins), jnp.float32)
    profile = jnp.concatenate([depth * cosine, depth * sine, unused], axis=0)
    drift = lax.dot_general(
        field[...].reshape(rows * half, bins),
        profile,
        (((1,), (1,)), ((), ())),
        precision=highest,
        preferred_element_type=jnp.float32,
    )
    drift_q[...] = drift.reshape(drift_q.shape)
    drift_moves = [
        Move(
            drift_q.at[pl.ds(tile_x * yy, tile_x)],
            drift_n.at[g, :, mine, :],
            init_send.at[6 + k],
            init_recv.at[6 + k],
            device,
            True,
            True,
        )
        for k, (yy, device) in enumerate(((y, at(1)), (1 - y, at(1, pair)), (1 - y, at(0, pair))))
    ]
    for m in drift_moves:
        m.start()
    back.start()
    spec_out[:, mine, :] = field[my_rows]
    drift_n[g, :, mine, :] = drift_q[my_rows]

    lane_n = iota((columns, LANES), 1)
    column_n = iota((tile_y, LANES), 0)

    def neighbours(k, array):
        result = []
        for r in range(tile_x):
            a = array[r]
            below = array[r - 1] if r > 0 else row_halo[k, 0]
            above = array[r + 1] if r < tile_x - 1 else row_halo[k, 1]
            lower = jnp.where(column_n == 0, col_halo[k, 0, r : r + 1, :], pltpu.roll(a, 1, 0))
            upper = jnp.where(column_n == tile_y - 1, col_halo[k, 1, r : r + 1, :], pltpu.roll(a, tile_y - 1, 0))
            result.append(above + below + upper + lower - 4.0 * a)
        return jnp.concatenate(result, axis=0)

    def swapped(a):
        from_v = pltpu.roll(a, LANES - NLEV, 1)
        from_u = pltpu.roll(a, NLEV, 1)
        return jnp.where(lane_n < NLEV, from_v, jnp.where(lane_n < 2 * NLEV, -from_u, 0.0))

    def ocean_section(array, laplace, drift_all):
        flat = array[...].reshape(columns, LANES)
        first = flat + ocean_step * (coriolis * swapped(flat + drift_all) + viscosity * laplace)
        return wet_n * (first + exact_dot(first, mix[...]))

    for m in sea_first:
        m.wait_recv()
    laplace_first = neighbours(0, ocean)
    for k, device in enumerate((at(1), at(1, pair), at(0, pair))):
        landing = drift_n.at[1 - g if k < 2 else g, :, mine if k == 0 else away, :]
        Move(drift_q.at[my_rows], landing, init_send.at[6 + k], init_recv.at[6 + k], device, True, True).wait_recv()
    drift_all = (drift_n[0] + drift_n[1]).reshape(columns, LANES)
    ocean_next[...] = ocean_section(ocean, laplace_first, drift_all).reshape(ocean.shape)
    set_col_edges(1, ocean_next)
    sea_second = sea_moves(1, ocean_next)
    for m in sea_second:
        m.start()

    def picking(offset):
        i, j = iota((LANES, own), 0), iota((LANES, own), 1)
        return jnp.where(i == j + own * g + offset, 1.0, 0.0)

    shape = u_out.shape
    pick_u, pick_v = picking(0), picking(NLEV)
    du_out[...] = exact_dot(drift_all, pick_u).reshape(shape)
    dv_out[...] = exact_dot(drift_all, pick_v).reshape(shape)
    for m in sea_second:
        m.wait_recv()
    final = ocean_section(ocean_next, neighbours(1, ocean_next), drift_all)
    u_out[...] = exact_dot(final, pick_u).reshape(shape)
    v_out[...] = exact_dot(final, pick_v).reshape(shape)
    back.wait_recv()
    for m in [to_grp, to_pair, flow_pair, back] + edges_flow + drift_moves + sea_first + sea_second:
        m.wait_send()


def solution(mesh):
    sizes = (mesh.shape["gx"], mesh.shape["gy"])
    theta = 2.0 * np.pi * np.arange(ND) / ND
    table = np.zeros((8, ND * NFL), np.float32)
    table[0] = np.repeat(np.cos(theta), NFL)
    table[1] = np.repeat(np.sin(theta), NFL)

    def body(spectrum, wet_mask, ocean_source, ocean_u, ocean_v, current_weights, drift_weights, inter_left, inter_right, inter_out, mixing):
        tile_x, tile_y, bins = spectrum.shape
        half, rows = tile_y // 2, 2 * tile_x
        own = ocean_u.shape[2]
        columns = tile_x * tile_y
        f32 = jnp.float32
        pack = jnp.concatenate(
            [
                ocean_u.reshape(columns, own),
                ocean_v.reshape(columns, own),
                wet_mask.astype(f32).reshape(columns, 1),
                ocean_source.astype(f32).reshape(columns, 1),
                jnp.zeros((columns, LANES - 2 * own - 2), f32),
            ],
            axis=1,
        )
        pack = jnp.concatenate([pack, jnp.pad(mixing, ((0, 0), (0, LANES - own)))], axis=0)
        low = NLEV
        cw = jnp.pad(current_weights, ((0, LANES - low), (0, LANES - NF))) + jnp.pad(
            current_weights, ((low, LANES - 2 * low), (NF, LANES - 2 * NF))
        )
        dw = jnp.pad(drift_weights, ((0, 64 - low), (0, LANES - NF)))[:low]
        vmem = pl.BlockSpec(memory_space=pltpu.VMEM)
        sea = (tile_x, tile_y, LANES)
        sections = WAVE_SECTIONS
        wave = (rows, half, bins)

        def V(*shape):
            return pltpu.VMEM(shape, f32)

        def D(*shape):
            return pltpu.SemaphoreType.DMA(shape)

        small = jax.ShapeDtypeStruct(ocean_u.shape, f32)
        return pl.pallas_call(
            functools.partial(kernel, sizes),
            out_shape=(jax.ShapeDtypeStruct(spectrum.shape, f32), small, small, small, small),
            in_specs=[vmem] * 8,
            out_specs=(vmem,) * 5,
            scratch_shapes=[
                V(tile_x, tile_y, bins),
                V(columns + NLEV, LANES),
                V(*sea),
                V(rows, half, LANES),
                V(2, 8, LANES),
                V(2, 8, LANES),
                V(*wave),
                V(sections, 2, 8, bins),
                V(sections, 2, 2, half, bins),
                V(sections, 2, 3, 8, bins),
                V(*wave),
                V(*wave),
                V(*wave),
                V(8, bins),
                V(8, bins),
                V(rows, half + 16, bins),
                V(*wave),
                V(LANES, LANES),
                V(*sea),
                V(*sea),
                V(2, 2, tile_y, LANES),
                V(2, 2, 8, LANES),
                V(2, 2, 8, LANES),
                V(rows, half, LANES),
                V(2, *sea),
                D(9),
                D(9),
                D(sections, 8),
                D(sections, 8),
                D(2, 4),
                D(2, 4),
            ],
            compiler_params=pltpu.CompilerParams(collective_id=0, has_side_effects=True, vmem_limit_bytes=40 * 2**20),
        )(spectrum, pack, jnp.asarray(table), cw, dw, inter_left, inter_right, inter_out)

    tile = P("gx", "gy", "grp")
    in_specs = (
        tile,
        P("gx", "gy"),
        P("gx", "gy"),
        tile,
        tile,
        P(),
        P(),
        P("grp", None),
        P("grp", None),
        P(None, "grp"),
        P(None, "grp"),
    )
    return jax.shard_map(body, mesh=mesh, in_specs=in_specs, out_specs=(tile,) * 5, check_vma=False)
```

```python
import functools

import jax
import jax.numpy as jnp
import numpy as np
from jax import lax
from jax.experimental import pallas as pl
from jax.experimental.pallas import tpu as pltpu
from jax.sharding import PartitionSpec as P

NF = 32
ND = 36
NLEV = 40
WAVE_SECTIONS = 3
NFL = 16
LANES = 128
MESH = pl.DeviceIdType.MESH

highest = lax.Precision.HIGHEST
inter_step = 0.1
ocean_step = 0.4
coriolis = 0.5
viscosity = 0.1


def exact_dot(a, b):
    return jnp.dot(a, b, precision=highest, preferred_element_type=jnp.float32)


def dot_on(a, b, dim_a, dim_b, precision=highest):
    return lax.dot_general(
        a, b, (((dim_a,), (dim_b,)), ((), ())), precision=precision, preferred_element_type=jnp.float32
    )


def sweep(centre, back_one, back_two, next_one, next_two, velocity):
    up = velocity >= 0.0
    one = jnp.where(up, back_one, next_one)
    two = jnp.where(up, back_two, next_two)
    size = jnp.abs(velocity)
    half = 0.5 * size
    return centre - half * (3.0 * centre - 4.0 * one + two) + half * size * (centre - 2.0 * one + two)


def iota(shape, dim):
    return lax.broadcasted_iota(jnp.int32, shape, dim)


class Move:
    def __init__(self, src, dst, send, recv, device, sends, receives):
        self.copy = pltpu.make_async_remote_copy(
            src_ref=src, dst_ref=dst, send_sem=send, recv_sem=recv, device_id=device, device_id_type=MESH
        )
        self.sends, self.receives = sends, receives

    def when(self, cond, act):
        if cond is True:
            act()
        else:
            pl.when(cond)(act)

    def start(self):
        self.when(self.sends, self.copy.start)

    def wait_send(self):
        self.when(self.sends, self.copy.wait_send)

    def wait_recv(self):
        self.when(self.receives, self.copy.wait_recv)


def kernel(
    sizes,
    spectrum_hbm,
    wet_mask,
    ocean_source,
    ocean_u,
    ocean_v,
    angles,
    cw,
    dw,
    left_hbm,
    right_hbm,
    out_hbm,
    mixing,
    spec_out,
    u_out,
    v_out,
    du_out,
    dv_out,
    spectrum,
    left,
    right,
    out_map,
    load_sem,
    pack,
    currents,
    masked,
    packs,
    own_flow,
    flow,
    flow_edge,
    flow_halo,
    field,
    edge,
    halo_x,
    halo_y,
    speed_x,
    speed_y,
    turn,
    speed_l,
    speed_r,
    wide,
    source,
    mix,
    ocean,
    ocean_next,
    row_halo,
    col_edge,
    col_halo,
    drift_q,
    drift_n,
    init_send,
    init_recv,
    wave_send,
    wave_recv,
    sea_send,
    sea_recv,
):
    nx, ny = sizes
    loads = [
        pltpu.make_async_copy(src, dst, load_sem.at[k])
        for k, (src, dst) in enumerate(
            ((spectrum_hbm, spectrum), (left_hbm, left), (right_hbm, right), (out_hbm, out_map))
        )
    ]
    for load in loads:
        load.start()
    tile_x, tile_y, bins = spectrum.shape
    half = tile_y // 2
    own = u_out.shape[0]
    rows = 2 * tile_x
    g, gx, gy = lax.axis_index("grp"), lax.axis_index("gx"), lax.axis_index("gy")
    z, y = gx // 2, gx % 2
    q = 2 * gy + y
    nz, nq = nx // 2, 2 * ny

    def at(dg=0, x=gx, c=gy):
        return {"grp": (g + dg) % 2, "gx": x, "gy": c}

    pair = 2 * z + 1 - y

    def q_at(dz, dq):
        qq = q + dq
        return at(0, 2 * (z + dz) + qq % 2, qq // 2)

    def inside(value, step, limit):
        return value + step >= 0 if step < 0 else value + step < limit

    def both(dz, dq):
        cond = inside(q, dq, nq)
        return cond if dz == 0 else cond & inside(z, dz, nz)

    friends = [(True, at(1)), (True, at(0, pair)), (True, at(1, pair))]
    friends += [(inside(z, d, nz), at(0, gx + 2 * d)) for d in (-1, 1)]
    friends += [(both(dz, dq), q_at(dz, dq)) for dq in (-1, 1) for dz in (-1, 0, 1)]
    friends += [(inside(gx, d, nx), at(0, gx + d)) for d in (-1, 1)]
    friends += [(inside(gy, d, ny), at(0, gx, gy + d)) for d in (-1, 1)]
    barrier = pltpu.get_barrier_semaphore()
    total = 0
    for cond, device in friends:

        def hello(device=device):
            pl.semaphore_signal(barrier, inc=1, device_id=device, device_id_type=MESH)

        if cond is True:
            hello()
            total = total + 1
        else:
            pl.when(cond)(hello)
            total = total + jnp.where(cond, 1, 0)

    columns = tile_x * tile_y

    def as_columns(table):
        ones = jnp.ones((1, LANES), jnp.float32)
        values = table[...].astype(jnp.float32)
        return jnp.concatenate([dot_on(values[r : r + 1], ones, 0, 0) for r in range(tile_x)], axis=0)

    place_i, place_j = iota((own, LANES), 0), iota((own, LANES), 1)
    place_u = jnp.where(place_j == place_i + own * g, 1.0, 0.0)
    place_v = jnp.where(place_j == place_i + own * g + NLEV, 1.0, 0.0)
    for r in range(tile_x):
        pack[r * tile_y : (r + 1) * tile_y] = dot_on(ocean_u[:, r, :], place_u, 0, 0) + dot_on(
            ocean_v[:, r, :], place_v, 0, 0
        )
    pack[columns:] = dot_on(mixing[...], place_u, 0, 0)
    wet_wide = as_columns(wet_mask)
    wet_n = wet_wide[:, 0:1]

    @pl.when(z == 0)
    def _():
        halo_x[:, 0] = jnp.zeros_like(halo_x[:, 0])

    @pl.when(z == nz - 1)
    def _():
        halo_x[:, 1] = jnp.zeros_like(halo_x[:, 1])

    for side, dq in ((0, -1), (1, 1)):

        @pl.when(jnp.logical_not(inside(q, dq, nq)))
        def _():
            halo_y[:, side] = jnp.zeros_like(halo_y[:, side])
            flow_halo[side] = jnp.zeros_like(flow_halo[side])

        for slot, dz in ((0, -1), (2, 1)):

            @pl.when(inside(q, dq, nq) & jnp.logical_not(inside(z, dz, nz)))
            def _():
                halo_y[:, side, slot] = jnp.zeros_like(halo_y[:, side, slot])

    for side, d in ((0, -1), (1, 1)):

        @pl.when(jnp.logical_not(inside(gx, d, nx)))
        def _():
            row_halo[:, side] = jnp.zeros_like(row_halo[:, side])

        @pl.when(jnp.logical_not(inside(gy, d, ny)))
        def _():
            col_halo[:, side] = jnp.zeros_like(col_halo[:, side])

    pl.semaphore_wait(barrier, total)

    to_grp = Move(pack, packs, init_send.at[0], init_recv.at[0], at(1), True, True)
    to_grp.start()
    loads[0].wait()
    masked[...] = (spectrum[...].reshape(columns, bins) * wet_n).reshape(tile_x, tile_y, bins)
    away = pl.ds(pl.multiple_of(half * (1 - y), 8), half)
    mine = pl.ds(pl.multiple_of(half * y, 8), half)
    my_rows = pl.ds(tile_x * y, tile_x)
    to_pair = Move(
        masked.at[:, away, :], field.at[my_rows], init_send.at[1], init_recv.at[1], at(0, pair), True, True
    )
    to_pair.start()
    field[my_rows] = masked[:, mine, :]

    chosen_at = as_columns(ocean_source)[:, 0:1]
    chosen = jnp.where(iota((columns, columns), 1).astype(jnp.float32) == chosen_at, 1.0, 0.0)
    currents[...] = jnp.zeros_like(currents)
    currents[0:NF, 0:NLEV] = cw[...]
    currents[NF : 2 * NF] = pltpu.roll(currents[0:NF], NLEV, 1)
    to_grp.wait_recv()
    everything = pack[...] + packs[...]
    ocean[...] = everything[:columns].reshape(ocean.shape)
    mix[...] = jnp.zeros_like(mix)
    mix[0:NLEV] = everything[columns:]
    mix[NLEV : 2 * NLEV] = pltpu.roll(everything[columns:], NLEV, 1)
    felt = exact_dot(chosen, dot_on(everything[:columns], currents[...], 1, 1))
    felt = felt + jnp.where(iota((columns, LANES), 1) == 2 * NF, wet_n, 0.0)
    own_flow[...] = felt.reshape(own_flow.shape)
    flow_pair = Move(
        own_flow.at[:, away, :], flow.at[my_rows], init_send.at[2], init_recv.at[2], at(0, pair), True, True
    )
    flow_pair.start()
    flow[my_rows] = own_flow[:, mine, :]

    def sea_moves(k, array):
        moves = []
        for side, d in ((0, -1), (1, 1)):
            moves.append(
                Move(
                    array.at[0 if d < 0 else tile_x - 1],
                    row_halo.at[k, 1 - side],
                    sea_send.at[k, side],
                    sea_recv.at[k, side],
                    at(0, gx + d),
                    inside(gx, d, nx),
                    inside(gx, -d, nx),
                )
            )
            moves.append(
                Move(
                    col_edge.at[k, side],
                    col_halo.at[k, 1 - side],
                    sea_send.at[k, 2 + side],
                    sea_recv.at[k, 2 + side],
                    at(0, gx, gy + d),
                    inside(gy, d, ny),
                    inside(gy, -d, ny),
                )
            )
        return moves

    def set_col_edges(k, array):
        for side, column in ((0, 0), (1, tile_y - 1)):
            for r in range(tile_x):
                col_edge[k, side, r : r + 1, :] = array[r, column : column + 1, :]

    lane = iota((1, bins), 1)
    frequency = (g * NFL + (lane & (NFL - 1))).astype(jnp.float32)
    group_speed = 0.2 + 0.4 * (NF - 1 - frequency) / (NF - 1)
    turning = 0.5 * (frequency + 1.0) / NF
    cosine, sine = angles[0:1, :], angles[1:2, :]
    spread_i = iota((LANES, bins), 0)
    spread_f = g * NFL + (iota((LANES, bins), 1) & (NFL - 1))
    spread_x = jnp.where(spread_i == spread_f, 1.0, 0.0)
    spread_y = jnp.where(spread_i == spread_f + NF, 1.0, 0.0)

    def wave_moves(s):
        moves = []
        for side, dz in ((0, -1), (1, 1)):
            moves.append(
                Move(
                    field.at[pl.ds(0 if dz < 0 else rows - 2, 2)],
                    halo_x.at[s, 1 - side],
                    wave_send.at[s, side],
                    wave_recv.at[s, side],
                    at(0, gx + 2 * dz),
                    inside(z, dz, nz),
                    inside(z, -dz, nz),
                )
            )
        k = 2
        for side, dq in ((0, -1), (1, 1)):
            for dz in (-1, 0, 1):
                moves.append(
                    Move(
                        edge.at[s, side],
                        halo_y.at[s, 1 - side, 1 - dz],
                        wave_send.at[s, k],
                        wave_recv.at[s, k],
                        q_at(dz, dq),
                        both(dz, dq),
                        both(-dz, -dq),
                    )
                )
                k += 1
        return moves

    def set_edges(s):
        for side, first in ((0, 0), (1, half - 2)):
            for r in range(rows):
                edge[s, side, 2 * r : 2 * r + 2, :] = field[r, first : first + 2, :]

    def interaction():
        now = field[...].reshape(rows * half, bins).astype(jnp.bfloat16)
        product = jnp.dot(now, left[...], preferred_element_type=jnp.float32) * jnp.dot(
            now, right[...], preferred_element_type=jnp.float32
        )
        result = dot_on(product.astype(jnp.bfloat16), out_map[...], 1, 1, None)
        source[...] = (inter_step * result).reshape(source.shape)

    def finish(s, moves):
        for m in moves:
            m.wait_recv()
        for side, speed, start in ((0, speed_l, 6), (1, speed_r, half + 8)):
            before, here, after = (halo_y[s, side, i] for i in range(3))
            low = iota((8, bins), 0)

            def joined(a, b, n):
                return jnp.where(low < n, pltpu.roll(a, n, 0), pltpu.roll(b, n, 0))

            packed = sweep(
                here,
                joined(before, here, 2),
                joined(before, here, 4),
                joined(here, after, 6),
                joined(here, after, 4),
                speed[...],
            )
            for r in range(rows):
                wide[r, start : start + 2, :] = packed[2 * r : 2 * r + 2]

        def line(r):
            if r < 0:
                return halo_x[s, 0, r + 2]
            if r >= rows:
                return halo_x[s, 1, r - rows]
            return field[r]

        for r in range(rows):
            wide[r, 8 : 8 + half, :] = sweep(
                line(r), line(r - 1), line(r - 2), line(r + 1), line(r + 2), speed_x[r]
            )
        for m in moves:
            m.wait_send()
        for r in range(rows):
            b = sweep(
                wide[r, 8 : 8 + half, :],
                wide[r, 7 : 7 + half, :],
                wide[r, 6 : 6 + half, :],
                wide[r, 9 : 9 + half, :],
                wide[r, 10 : 10 + half, :],
                speed_y[r],
            )
            t = turn[r]
            behind = jnp.concatenate([b[:, bins - NFL :], b[:, : bins - NFL]], axis=1)
            ahead = jnp.concatenate([b[:, NFL:], b[:, :NFL]], axis=1)
            c = b - jnp.abs(t) * (b - jnp.where(t >= 0.0, behind, ahead))
            field[r] = flow[r, :, 2 * NF : 2 * NF + 1] * (c + source[r])

    def flow_moves():
        return [
            Move(
                flow_edge.at[side],
                flow_halo.at[1 - side],
                init_send.at[3 + side],
                init_recv.at[3 + side],
                q_at(0, dq),
                inside(q, dq, nq),
                inside(q, -dq, nq),
            )
            for side, dq in ((0, -1), (1, 1))
        ]

    to_pair.wait_recv()
    set_edges(0)
    first_moves = wave_moves(0)
    for m in first_moves:
        m.start()
    set_col_edges(0, ocean)
    flow_pair.wait_recv()
    for side, first in ((0, 0), (1, half - 2)):
        for r in range(rows):
            flow_edge[side, 2 * r : 2 * r + 2, :] = flow[r, first : first + 2, :]
    edges_flow = flow_moves()
    for m in edges_flow:
        m.start()
    sea_first = sea_moves(0, ocean)
    for m in sea_first:
        m.start()
    fq = flow[...].reshape(rows * half, LANES)
    fx = exact_dot(fq, spread_x)
    fy = exact_dot(fq, spread_y)
    speed_x[...] = (group_speed * cosine + fx).reshape(speed_x.shape)
    speed_y[...] = (group_speed * sine + fy).reshape(speed_x.shape)
    turn[...] = (turning * (sine * fx - cosine * fy)).reshape(speed_x.shape)
    for load in loads[1:]:
        load.wait()
    interaction()
    for m in edges_flow:
        m.wait_recv()
    speed_l[...] = group_speed * cosine + exact_dot(flow_halo[0], spread_x)
    speed_r[...] = group_speed * cosine + exact_dot(flow_halo[1], spread_x)
    finish(0, first_moves)

    def section(s, carry):
        set_edges(s)
        moves = wave_moves(s)
        for m in moves:
            m.start()
        interaction()
        finish(s, moves)
        return carry

    lax.fori_loop(1, WAVE_SECTIONS, section, 0)

    their_rows = pl.ds(tile_x * (1 - y), tile_x)
    back = Move(
        field.at[their_rows], spec_out.at[:, mine, :], init_send.at[5], init_recv.at[5], at(0, pair), True, True
    )
    depth = dot_on(dw[...], spread_x[0:NF], 0, 0)
    unused = jnp.zeros((LANES - 2 * NLEV, bins), jnp.float32)
    profile = jnp.concatenate([depth * cosine, depth * sine, unused], axis=0)
    drift = lax.dot_general(
        field[...].reshape(rows * half, bins),
        profile,
        (((1,), (1,)), ((), ())),
        precision=highest,
        preferred_element_type=jnp.float32,
    )
    drift_q[...] = drift.reshape(drift_q.shape)
    drift_moves = [
        Move(
            drift_q.at[pl.ds(tile_x * yy, tile_x)],
            drift_n.at[g, :, mine, :],
            init_send.at[6 + k],
            init_recv.at[6 + k],
            device,
            True,
            True,
        )
        for k, (yy, device) in enumerate(((y, at(1)), (1 - y, at(1, pair)), (1 - y, at(0, pair))))
    ]
    for m in drift_moves:
        m.start()
    back.start()
    spec_out[:, mine, :] = field[my_rows]
    drift_n[g, :, mine, :] = drift_q[my_rows]

    lane_n = iota((columns, LANES), 1)
    column_n = iota((tile_y, LANES), 0)

    def neighbours(k, array):
        result = []
        for r in range(tile_x):
            a = array[r]
            below = array[r - 1] if r > 0 else row_halo[k, 0]
            above = array[r + 1] if r < tile_x - 1 else row_halo[k, 1]
            lower = jnp.where(column_n == 0, col_halo[k, 0, r : r + 1, :], pltpu.roll(a, 1, 0))
            upper = jnp.where(column_n == tile_y - 1, col_halo[k, 1, r : r + 1, :], pltpu.roll(a, tile_y - 1, 0))
            result.append(above + below + upper + lower - 4.0 * a)
        return jnp.concatenate(result, axis=0)

    def swapped(a):
        from_v = pltpu.roll(a, LANES - NLEV, 1)
        from_u = pltpu.roll(a, NLEV, 1)
        return jnp.where(lane_n < NLEV, from_v, jnp.where(lane_n < 2 * NLEV, -from_u, 0.0))

    def ocean_section(array, laplace, drift_all):
        flat = array[...].reshape(columns, LANES)
        first = flat + ocean_step * (coriolis * swapped(flat + drift_all) + viscosity * laplace)
        return wet_n * (first + exact_dot(first, mix[...]))

    for m in sea_first:
        m.wait_recv()
    laplace_first = neighbours(0, ocean)
    for k, device in enumerate((at(1), at(1, pair), at(0, pair))):
        landing = drift_n.at[1 - g if k < 2 else g, :, mine if k == 0 else away, :]
        Move(drift_q.at[my_rows], landing, init_send.at[6 + k], init_recv.at[6 + k], device, True, True).wait_recv()
    drift_all = (drift_n[0] + drift_n[1]).reshape(columns, LANES)
    ocean_next[...] = ocean_section(ocean, laplace_first, drift_all).reshape(ocean.shape)
    set_col_edges(1, ocean_next)
    sea_second = sea_moves(1, ocean_next)
    for m in sea_second:
        m.start()

    def picking(offset):
        i, j = iota((LANES, own), 0), iota((LANES, own), 1)
        return jnp.where(i == j + own * g + offset, 1.0, 0.0)

    pick_u, pick_v = picking(0), picking(NLEV)

    def give(out, pick, values):
        for r in range(tile_x):
            out[:, r, :] = dot_on(pick, values[r * tile_y : (r + 1) * tile_y], 0, 1)

    give(du_out, pick_u, drift_all)
    give(dv_out, pick_v, drift_all)
    for m in sea_second:
        m.wait_recv()
    final = ocean_section(ocean_next, neighbours(1, ocean_next), drift_all)
    give(u_out, pick_u, final)
    give(v_out, pick_v, final)
    back.wait_recv()
    for m in [to_grp, to_pair, flow_pair, back] + edges_flow + drift_moves + sea_first + sea_second:
        m.wait_send()


def store_kernel(*refs):
    count = (len(refs) - 1) // 2
    copies = [pltpu.make_async_copy(refs[i], refs[count + i], refs[-1].at[i]) for i in range(count)]
    for copy in copies:
        copy.start()
    for copy in copies:
        copy.wait()


def solution(mesh):
    sizes = (mesh.shape["gx"], mesh.shape["gy"])
    theta = 2.0 * np.pi * np.arange(ND) / ND
    table = np.zeros((8, ND * NFL), np.float32)
    table[0] = np.repeat(np.cos(theta), NFL)
    table[1] = np.repeat(np.sin(theta), NFL)

    def body(spectrum, wet_mask, ocean_source, ocean_u, ocean_v, current_weights, drift_weights, inter_left, inter_right, inter_out, mixing):
        tile_x, tile_y, bins = spectrum.shape
        half, rows = tile_y // 2, 2 * tile_x
        own = ocean_u.shape[2]
        columns = tile_x * tile_y
        f32 = jnp.float32
        vmem = pl.BlockSpec(memory_space=pltpu.VMEM)
        sea = (tile_x, tile_y, LANES)
        sections = WAVE_SECTIONS
        wave = (rows, half, bins)

        def V(*shape):
            return pltpu.VMEM(shape, f32)

        def D(*shape):
            return pltpu.SemaphoreType.DMA(shape)

        outs = (jax.ShapeDtypeStruct(spectrum.shape, f32),) + (
            jax.ShapeDtypeStruct((own, tile_x, tile_y), f32),
        ) * 4
        anywhere = pl.BlockSpec(memory_space=pl.ANY)
        results = pl.pallas_call(
            functools.partial(kernel, sizes),
            out_shape=outs,
            in_specs=[anywhere] + [vmem] * 7 + [anywhere] * 3 + [vmem],
            out_specs=(vmem,) * 5,
            scratch_shapes=[
                V(tile_x, tile_y, bins),
                pltpu.VMEM(inter_left.shape, inter_left.dtype),
                pltpu.VMEM(inter_right.shape, inter_right.dtype),
                pltpu.VMEM(inter_out.shape[::-1], inter_out.dtype),
                D(4),
                V(columns + NLEV, LANES),
                V(LANES, LANES),
                V(tile_x, tile_y, bins),
                V(columns + NLEV, LANES),
                V(*sea),
                V(rows, half, LANES),
                V(2, 8, LANES),
                V(2, 8, LANES),
                V(*wave),
                V(sections, 2, 8, bins),
                V(sections, 2, 2, half, bins),
                V(sections, 2, 3, 8, bins),
                V(*wave),
                V(*wave),
                V(*wave),
                V(8, bins),
                V(8, bins),
                V(rows, half + 16, bins),
                V(*wave),
                V(LANES, LANES),
                V(*sea),
                V(*sea),
                V(2, 2, tile_y, LANES),
                V(2, 2, 8, LANES),
                V(2, 2, 8, LANES),
                V(rows, half, LANES),
                V(2, *sea),
                D(9),
                D(9),
                D(sections, 8),
                D(sections, 8),
                D(2, 4),
                D(2, 4),
            ],
            compiler_params=pltpu.CompilerParams(collective_id=0, has_side_effects=True),
        )(
            spectrum,
            wet_mask,
            ocean_source,
            jnp.transpose(ocean_u, (2, 0, 1)),
            jnp.transpose(ocean_v, (2, 0, 1)),
            jnp.asarray(table),
            current_weights.T,
            drift_weights.T,
            inter_left,
            inter_right,
            inter_out.T,
            mixing.T,
        )
        results = pl.pallas_call(
            store_kernel,
            out_shape=outs,
            in_specs=[vmem] * 5,
            out_specs=(anywhere,) * 5,
            scratch_shapes=[D(5)],
        )(*results)
        return (results[0],) + tuple(jnp.transpose(a, (1, 2, 0)) for a in results[1:])

    tile = P("gx", "gy", "grp")
    in_specs = (
        tile,
        P("gx", "gy"),
        P("gx", "gy"),
        tile,
        tile,
        P(),
        P(),
        P("grp", None),
        P("grp", None),
        P(None, "grp"),
        P(None, "grp"),
    )
    return jax.shard_map(body, mesh=mesh, in_specs=in_specs, out_specs=(tile,) * 5, check_vma=False)
```

```python
import functools

import jax
import jax.numpy as jnp
import numpy as np
from jax import lax
from jax.experimental import pallas as pl
from jax.experimental.pallas import tpu as pltpu
from jax.sharding import PartitionSpec as P

NF = 32
ND = 36
NLEV = 40
WAVE_SECTIONS = 3
NFL = 16
LANES = 128
MESH = pl.DeviceIdType.MESH

highest = lax.Precision.HIGHEST
inter_step = 0.1
ocean_step = 0.4
coriolis = 0.5
viscosity = 0.1


def exact_dot(a, b):
    return jnp.dot(a, b, precision=highest, preferred_element_type=jnp.float32)


def dot_on(a, b, dim_a, dim_b, precision=highest):
    return lax.dot_general(
        a, b, (((dim_a,), (dim_b,)), ((), ())), precision=precision, preferred_element_type=jnp.float32
    )


def sweep(centre, back_one, back_two, next_one, next_two, velocity):
    up = velocity >= 0.0
    one = jnp.where(up, back_one, next_one)
    two = jnp.where(up, back_two, next_two)
    size = jnp.abs(velocity)
    half = 0.5 * size
    return centre - half * (3.0 * centre - 4.0 * one + two) + half * size * (centre - 2.0 * one + two)


def iota(shape, dim):
    return lax.broadcasted_iota(jnp.int32, shape, dim)


class Move:
    def __init__(self, src, dst, send, recv, device, sends, receives):
        self.copy = pltpu.make_async_remote_copy(
            src_ref=src, dst_ref=dst, send_sem=send, recv_sem=recv, device_id=device, device_id_type=MESH
        )
        self.sends, self.receives = sends, receives

    def when(self, cond, act):
        if cond is True:
            act()
        else:
            pl.when(cond)(act)

    def start(self):
        self.when(self.sends, self.copy.start)

    def wait_send(self):
        self.when(self.sends, self.copy.wait_send)

    def wait_recv(self):
        self.when(self.receives, self.copy.wait_recv)


def kernel(
    sizes,
    spectrum_hbm,
    wet_mask,
    ocean_source,
    ocean_u,
    ocean_v,
    angles,
    cw,
    dw,
    left_hbm,
    right_hbm,
    out_hbm,
    mixing,
    spec_out,
    u_out,
    v_out,
    du_out,
    dv_out,
    spectrum,
    left,
    right,
    out_map,
    load_sem,
    pack,
    currents,
    masked,
    packs,
    own_flow,
    flow,
    flow_edge,
    flow_halo,
    field,
    edge,
    halo_x,
    halo_y,
    speed_x,
    speed_y,
    turn,
    speed_l,
    speed_r,
    wide,
    source,
    mix,
    ocean,
    ocean_next,
    row_halo,
    col_edge,
    col_halo,
    drift_q,
    drift_n,
    init_send,
    init_recv,
    wave_send,
    wave_recv,
    sea_send,
    sea_recv,
):
    nx, ny = sizes
    loads = [
        pltpu.make_async_copy(src, dst, load_sem.at[k])
        for k, (src, dst) in enumerate(
            ((spectrum_hbm, spectrum), (left_hbm, left), (right_hbm, right), (out_hbm, out_map))
        )
    ]
    for load in loads:
        load.start()
    tile_x, tile_y, bins = spectrum.shape
    half = tile_y // 2
    own = u_out.shape[0]
    rows = 2 * tile_x
    g, gx, gy = lax.axis_index("grp"), lax.axis_index("gx"), lax.axis_index("gy")
    z, y = gx // 2, gx % 2
    q = 2 * gy + y
    nz, nq = nx // 2, 2 * ny

    def at(dg=0, x=gx, c=gy):
        return {"grp": (g + dg) % 2, "gx": x, "gy": c}

    pair = 2 * z + 1 - y

    def q_at(dz, dq):
        qq = q + dq
        return at(0, 2 * (z + dz) + qq % 2, qq // 2)

    def inside(value, step, limit):
        return value + step >= 0 if step < 0 else value + step < limit

    def both(dz, dq):
        cond = inside(q, dq, nq)
        return cond if dz == 0 else cond & inside(z, dz, nz)

    friends = [(True, at(1)), (True, at(0, pair)), (True, at(1, pair))]
    friends += [(inside(z, d, nz), at(0, gx + 2 * d)) for d in (-1, 1)]
    friends += [(both(dz, dq), q_at(dz, dq)) for dq in (-1, 1) for dz in (-1, 0, 1)]
    friends += [(inside(gx, d, nx), at(0, gx + d)) for d in (-1, 1)]
    friends += [(inside(gy, d, ny), at(0, gx, gy + d)) for d in (-1, 1)]
    barrier = pltpu.get_barrier_semaphore()
    total = 0
    for cond, device in friends:

        def hello(device=device):
            pl.semaphore_signal(barrier, inc=1, device_id=device, device_id_type=MESH)

        if cond is True:
            hello()
            total = total + 1
        else:
            pl.when(cond)(hello)
            total = total + jnp.where(cond, 1, 0)

    columns = tile_x * tile_y

    def as_columns(table):
        ones = jnp.ones((1, LANES), jnp.float32)
        values = table[...].astype(jnp.float32)
        return jnp.concatenate([dot_on(values[r : r + 1], ones, 0, 0) for r in range(tile_x)], axis=0)

    place_i, place_j = iota((own, LANES), 0), iota((own, LANES), 1)
    place_u = jnp.where(place_j == place_i + own * g, 1.0, 0.0)
    place_v = jnp.where(place_j == place_i + own * g + NLEV, 1.0, 0.0)
    for r in range(tile_x):
        pack[r * tile_y : (r + 1) * tile_y] = dot_on(ocean_u[:, r, :], place_u, 0, 0) + dot_on(
            ocean_v[:, r, :], place_v, 0, 0
        )
    pack[columns:] = dot_on(mixing[...], place_u, 0, 0)
    wet_wide = as_columns(wet_mask)
    wet_n = wet_wide[:, 0:1]

    @pl.when(z == 0)
    def _():
        halo_x[:, 0] = jnp.zeros_like(halo_x[:, 0])

    @pl.when(z == nz - 1)
    def _():
        halo_x[:, 1] = jnp.zeros_like(halo_x[:, 1])

    for side, dq in ((0, -1), (1, 1)):

        @pl.when(jnp.logical_not(inside(q, dq, nq)))
        def _():
            halo_y[:, side] = jnp.zeros_like(halo_y[:, side])
            flow_halo[side] = jnp.zeros_like(flow_halo[side])

        for slot, dz in ((0, -1), (2, 1)):

            @pl.when(inside(q, dq, nq) & jnp.logical_not(inside(z, dz, nz)))
            def _():
                halo_y[:, side, slot] = jnp.zeros_like(halo_y[:, side, slot])

    for side, d in ((0, -1), (1, 1)):

        @pl.when(jnp.logical_not(inside(gx, d, nx)))
        def _():
            row_halo[:, side] = jnp.zeros_like(row_halo[:, side])

        @pl.when(jnp.logical_not(inside(gy, d, ny)))
        def _():
            col_halo[:, side] = jnp.zeros_like(col_halo[:, side])

    loads[0].wait()
    masked[...] = (spectrum[...].reshape(columns, bins) * wet_n).reshape(tile_x, tile_y, bins)

    pl.semaphore_wait(barrier, total)

    to_grp = Move(pack, packs, init_send.at[0], init_recv.at[0], at(1), True, True)
    to_grp.start()
    away = pl.ds(pl.multiple_of(half * (1 - y), 8), half)
    mine = pl.ds(pl.multiple_of(half * y, 8), half)
    my_rows = pl.ds(tile_x * y, tile_x)
    to_pair = Move(
        masked.at[:, away, :], field.at[my_rows], init_send.at[1], init_recv.at[1], at(0, pair), True, True
    )
    to_pair.start()
    field[my_rows] = masked[:, mine, :]

    def wave_moves(s):
        moves = []
        for side, dz in ((0, -1), (1, 1)):
            moves.append(
                Move(
                    field.at[pl.ds(0 if dz < 0 else rows - 2, 2)],
                    halo_x.at[s, 1 - side],
                    wave_send.at[s, side],
                    wave_recv.at[s, side],
                    at(0, gx + 2 * dz),
                    inside(z, dz, nz),
                    inside(z, -dz, nz),
                )
            )
        k = 2
        for side, dq in ((0, -1), (1, 1)):
            for dz in (-1, 0, 1):
                moves.append(
                    Move(
                        edge.at[s, side],
                        halo_y.at[s, 1 - side, 1 - dz],
                        wave_send.at[s, k],
                        wave_recv.at[s, k],
                        q_at(dz, dq),
                        both(dz, dq),
                        both(-dz, -dq),
                    )
                )
                k += 1
        return moves

    first_moves = wave_moves(0)
    pl.when(y == 0)(first_moves[0].start)
    pl.when(y == 1)(first_moves[1].start)

    chosen_at = as_columns(ocean_source)[:, 0:1]
    chosen = jnp.where(iota((columns, columns), 1).astype(jnp.float32) == chosen_at, 1.0, 0.0)
    currents[...] = jnp.zeros_like(currents)
    currents[0:NF, 0:NLEV] = cw[...]
    currents[NF : 2 * NF] = pltpu.roll(currents[0:NF], NLEV, 1)
    to_grp.wait_recv()
    everything = pack[...] + packs[...]
    ocean[...] = everything[:columns].reshape(ocean.shape)
    mix[...] = jnp.zeros_like(mix)
    mix[0:NLEV] = everything[columns:]
    mix[NLEV : 2 * NLEV] = pltpu.roll(everything[columns:], NLEV, 1)
    felt = exact_dot(chosen, dot_on(everything[:columns], currents[...], 1, 1))
    felt = felt + jnp.where(iota((columns, LANES), 1) == 2 * NF, wet_n, 0.0)
    own_flow[...] = felt.reshape(own_flow.shape)
    flow_pair = Move(
        own_flow.at[:, away, :], flow.at[my_rows], init_send.at[2], init_recv.at[2], at(0, pair), True, True
    )
    flow_pair.start()
    flow[my_rows] = own_flow[:, mine, :]

    def sea_moves(k, array):
        moves = []
        for side, d in ((0, -1), (1, 1)):
            moves.append(
                Move(
                    array.at[0 if d < 0 else tile_x - 1],
                    row_halo.at[k, 1 - side],
                    sea_send.at[k, side],
                    sea_recv.at[k, side],
                    at(0, gx + d),
                    inside(gx, d, nx),
                    inside(gx, -d, nx),
                )
            )
            moves.append(
                Move(
                    col_edge.at[k, side],
                    col_halo.at[k, 1 - side],
                    sea_send.at[k, 2 + side],
                    sea_recv.at[k, 2 + side],
                    at(0, gx, gy + d),
                    inside(gy, d, ny),
                    inside(gy, -d, ny),
                )
            )
        return moves

    def set_col_edges(k, array):
        for side, column in ((0, 0), (1, tile_y - 1)):
            for r in range(tile_x):
                col_edge[k, side, r : r + 1, :] = array[r, column : column + 1, :]

    lane = iota((1, bins), 1)
    frequency = (g * NFL + (lane & (NFL - 1))).astype(jnp.float32)
    group_speed = 0.2 + 0.4 * (NF - 1 - frequency) / (NF - 1)
    turning = 0.5 * (frequency + 1.0) / NF
    cosine, sine = angles[0:1, :], angles[1:2, :]
    spread_i = iota((LANES, bins), 0)
    spread_f = g * NFL + (iota((LANES, bins), 1) & (NFL - 1))
    spread_x = jnp.where(spread_i == spread_f, 1.0, 0.0)
    spread_y = jnp.where(spread_i == spread_f + NF, 1.0, 0.0)

    def set_edges(s):
        for side, first in ((0, 0), (1, half - 2)):
            for r in range(rows):
                edge[s, side, 2 * r : 2 * r + 2, :] = field[r, first : first + 2, :]

    def interaction():
        now = field[...].reshape(rows * half, bins).astype(jnp.bfloat16)
        product = jnp.dot(now, left[...], preferred_element_type=jnp.float32) * jnp.dot(
            now, right[...], preferred_element_type=jnp.float32
        )
        result = dot_on(product.astype(jnp.bfloat16), out_map[...], 1, 1, None)
        source[...] = (inter_step * result).reshape(source.shape)

    def finish(s, moves):
        for m in moves:
            m.wait_recv()
        for side, speed, start in ((0, speed_l, 6), (1, speed_r, half + 8)):
            before, here, after = (halo_y[s, side, i] for i in range(3))
            low = iota((8, bins), 0)

            def joined(a, b, n):
                return jnp.where(low < n, pltpu.roll(a, n, 0), pltpu.roll(b, n, 0))

            packed = sweep(
                here,
                joined(before, here, 2),
                joined(before, here, 4),
                joined(here, after, 6),
                joined(here, after, 4),
                speed[...],
            )
            for r in range(rows):
                wide[r, start : start + 2, :] = packed[2 * r : 2 * r + 2]

        def line(r):
            if r < 0:
                return halo_x[s, 0, r + 2]
            if r >= rows:
                return halo_x[s, 1, r - rows]
            return field[r]

        for r in range(rows):
            wide[r, 8 : 8 + half, :] = sweep(
                line(r), line(r - 1), line(r - 2), line(r + 1), line(r + 2), speed_x[r]
            )
        for m in moves:
            m.wait_send()
        for r in range(rows):
            b = sweep(
                wide[r, 8 : 8 + half, :],
                wide[r, 7 : 7 + half, :],
                wide[r, 6 : 6 + half, :],
                wide[r, 9 : 9 + half, :],
                wide[r, 10 : 10 + half, :],
                speed_y[r],
            )
            t = turn[r]
            behind = jnp.concatenate([b[:, bins - NFL :], b[:, : bins - NFL]], axis=1)
            ahead = jnp.concatenate([b[:, NFL:], b[:, :NFL]], axis=1)
            c = b - jnp.abs(t) * (b - jnp.where(t >= 0.0, behind, ahead))
            field[r] = flow[r, :, 2 * NF : 2 * NF + 1] * (c + source[r])

    def flow_moves():
        return [
            Move(
                flow_edge.at[side],
                flow_halo.at[1 - side],
                init_send.at[3 + side],
                init_recv.at[3 + side],
                q_at(0, dq),
                inside(q, dq, nq),
                inside(q, -dq, nq),
            )
            for side, dq in ((0, -1), (1, 1))
        ]

    to_pair.wait_recv()
    set_edges(0)
    for m in first_moves[2:]:
        m.start()
    pl.when(y == 1)(first_moves[0].start)
    pl.when(y == 0)(first_moves[1].start)
    set_col_edges(0, ocean)
    flow_pair.wait_recv()
    for side, first in ((0, 0), (1, half - 2)):
        for r in range(rows):
            flow_edge[side, 2 * r : 2 * r + 2, :] = flow[r, first : first + 2, :]
    edges_flow = flow_moves()
    for m in edges_flow:
        m.start()
    sea_first = sea_moves(0, ocean)
    for m in sea_first:
        m.start()
    fq = flow[...].reshape(rows * half, LANES)
    fx = exact_dot(fq, spread_x)
    fy = exact_dot(fq, spread_y)
    speed_x[...] = (group_speed * cosine + fx).reshape(speed_x.shape)
    speed_y[...] = (group_speed * sine + fy).reshape(speed_x.shape)
    turn[...] = (turning * (sine * fx - cosine * fy)).reshape(speed_x.shape)
    for load in loads[1:]:
        load.wait()
    interaction()
    for m in edges_flow:
        m.wait_recv()
    speed_l[...] = group_speed * cosine + exact_dot(flow_halo[0], spread_x)
    speed_r[...] = group_speed * cosine + exact_dot(flow_halo[1], spread_x)
    finish(0, first_moves)

    def section(s, carry):
        set_edges(s)
        moves = wave_moves(s)
        for m in moves[2:] + moves[:2]:
            m.start()
        interaction()
        finish(s, moves)
        return carry

    lax.fori_loop(1, WAVE_SECTIONS, section, 0)

    their_rows = pl.ds(tile_x * (1 - y), tile_x)
    back = Move(
        field.at[their_rows], spec_out.at[:, mine, :], init_send.at[5], init_recv.at[5], at(0, pair), True, True
    )
    depth = dot_on(dw[...], spread_x[0:NF], 0, 0)
    unused = jnp.zeros((LANES - 2 * NLEV, bins), jnp.float32)
    profile = jnp.concatenate([depth * cosine, depth * sine, unused], axis=0)
    drift = lax.dot_general(
        field[...].reshape(rows * half, bins),
        profile,
        (((1,), (1,)), ((), ())),
        precision=highest,
        preferred_element_type=jnp.float32,
    )
    drift_q[...] = drift.reshape(drift_q.shape)
    drift_moves = [
        Move(
            drift_q.at[pl.ds(tile_x * yy, tile_x)],
            drift_n.at[g, :, mine, :],
            init_send.at[6 + k],
            init_recv.at[6 + k],
            device,
            True,
            True,
        )
        for k, (yy, device) in enumerate(((y, at(1)), (1 - y, at(1, pair)), (1 - y, at(0, pair))))
    ]
    for m in drift_moves:
        m.start()
    back.start()
    spec_out[:, mine, :] = field[my_rows]
    drift_n[g, :, mine, :] = drift_q[my_rows]

    lane_n = iota((columns, LANES), 1)
    column_n = iota((tile_y, LANES), 0)

    def neighbours(k, array):
        result = []
        for r in range(tile_x):
            a = array[r]
            below = array[r - 1] if r > 0 else row_halo[k, 0]
            above = array[r + 1] if r < tile_x - 1 else row_halo[k, 1]
            lower = jnp.where(column_n == 0, col_halo[k, 0, r : r + 1, :], pltpu.roll(a, 1, 0))
            upper = jnp.where(column_n == tile_y - 1, col_halo[k, 1, r : r + 1, :], pltpu.roll(a, tile_y - 1, 0))
            result.append(above + below + upper + lower - 4.0 * a)
        return jnp.concatenate(result, axis=0)

    def swapped(a):
        from_v = pltpu.roll(a, LANES - NLEV, 1)
        from_u = pltpu.roll(a, NLEV, 1)
        return jnp.where(lane_n < NLEV, from_v, jnp.where(lane_n < 2 * NLEV, -from_u, 0.0))

    def ocean_section(array, laplace, drift_all):
        flat = array[...].reshape(columns, LANES)
        first = flat + ocean_step * (coriolis * swapped(flat + drift_all) + viscosity * laplace)
        return wet_n * (first + exact_dot(first, mix[...]))

    for m in sea_first:
        m.wait_recv()
    laplace_first = neighbours(0, ocean)
    for k, device in enumerate((at(1), at(1, pair), at(0, pair))):
        landing = drift_n.at[1 - g if k < 2 else g, :, mine if k == 0 else away, :]
        Move(drift_q.at[my_rows], landing, init_send.at[6 + k], init_recv.at[6 + k], device, True, True).wait_recv()
    drift_all = (drift_n[0] + drift_n[1]).reshape(columns, LANES)
    ocean_next[...] = ocean_section(ocean, laplace_first, drift_all).reshape(ocean.shape)
    set_col_edges(1, ocean_next)
    sea_second = sea_moves(1, ocean_next)
    for m in sea_second:
        m.start()

    def picking(offset):
        i, j = iota((LANES, own), 0), iota((LANES, own), 1)
        return jnp.where(i == j + own * g + offset, 1.0, 0.0)

    pick_u, pick_v = picking(0), picking(NLEV)

    def give(out, pick, values):
        for r in range(tile_x):
            out[:, r, :] = dot_on(pick, values[r * tile_y : (r + 1) * tile_y], 0, 1)

    give(du_out, pick_u, drift_all)
    give(dv_out, pick_v, drift_all)
    for m in sea_second:
        m.wait_recv()
    final = ocean_section(ocean_next, neighbours(1, ocean_next), drift_all)
    give(u_out, pick_u, final)
    give(v_out, pick_v, final)
    back.wait_recv()
    for m in [to_grp, to_pair, flow_pair, back] + edges_flow + drift_moves + sea_first + sea_second:
        m.wait_send()


def store_kernel(*refs):
    count = (len(refs) - 1) // 2
    copies = [pltpu.make_async_copy(refs[i], refs[count + i], refs[-1].at[i]) for i in range(count)]
    for copy in copies:
        copy.start()
    for copy in copies:
        copy.wait()


def solution(mesh):
    sizes = (mesh.shape["gx"], mesh.shape["gy"])
    theta = 2.0 * np.pi * np.arange(ND) / ND
    table = np.zeros((8, ND * NFL), np.float32)
    table[0] = np.repeat(np.cos(theta), NFL)
    table[1] = np.repeat(np.sin(theta), NFL)

    def body(spectrum, wet_mask, ocean_source, ocean_u, ocean_v, current_weights, drift_weights, inter_left, inter_right, inter_out, mixing):
        tile_x, tile_y, bins = spectrum.shape
        half, rows = tile_y // 2, 2 * tile_x
        own = ocean_u.shape[2]
        columns = tile_x * tile_y
        f32 = jnp.float32
        vmem = pl.BlockSpec(memory_space=pltpu.VMEM)
        sea = (tile_x, tile_y, LANES)
        sections = WAVE_SECTIONS
        wave = (rows, half, bins)

        def V(*shape):
            return pltpu.VMEM(shape, f32)

        def D(*shape):
            return pltpu.SemaphoreType.DMA(shape)

        outs = (jax.ShapeDtypeStruct(spectrum.shape, f32),) + (
            jax.ShapeDtypeStruct((own, tile_x, tile_y), f32),
        ) * 4
        anywhere = pl.BlockSpec(memory_space=pl.ANY)
        results = pl.pallas_call(
            functools.partial(kernel, sizes),
            out_shape=tuple(pltpu.VMEM(a.shape, a.dtype) for a in outs),
            in_specs=[anywhere] + [vmem] * 7 + [anywhere] * 3 + [vmem],
            out_specs=(vmem,) * 5,
            scratch_shapes=[
                V(tile_x, tile_y, bins),
                pltpu.VMEM(inter_left.shape, inter_left.dtype),
                pltpu.VMEM(inter_right.shape, inter_right.dtype),
                pltpu.VMEM(inter_out.shape[::-1], inter_out.dtype),
                D(4),
                V(columns + NLEV, LANES),
                V(LANES, LANES),
                V(tile_x, tile_y, bins),
                V(columns + NLEV, LANES),
                V(*sea),
                V(rows, half, LANES),
                V(2, 8, LANES),
                V(2, 8, LANES),
                V(*wave),
                V(sections, 2, 8, bins),
                V(sections, 2, 2, half, bins),
                V(sections, 2, 3, 8, bins),
                V(*wave),
                V(*wave),
                V(*wave),
                V(8, bins),
                V(8, bins),
                V(rows, half + 16, bins),
                V(*wave),
                V(LANES, LANES),
                V(*sea),
                V(*sea),
                V(2, 2, tile_y, LANES),
                V(2, 2, 8, LANES),
                V(2, 2, 8, LANES),
                V(rows, half, LANES),
                V(2, *sea),
                D(9),
                D(9),
                D(sections, 8),
                D(sections, 8),
                D(2, 4),
                D(2, 4),
            ],
            compiler_params=pltpu.CompilerParams(collective_id=0, has_side_effects=True),
        )(
            spectrum,
            wet_mask,
            ocean_source,
            jnp.transpose(ocean_u, (2, 0, 1)),
            jnp.transpose(ocean_v, (2, 0, 1)),
            jnp.asarray(table),
            current_weights.T,
            drift_weights.T,
            inter_left,
            inter_right,
            inter_out.T,
            mixing.T,
        )
        results = pl.pallas_call(
            store_kernel,
            out_shape=outs,
            in_specs=[anywhere] * 5,
            out_specs=(anywhere,) * 5,
            scratch_shapes=[D(5)],
        )(*(pltpu.with_memory_space_constraint(a, pltpu.VMEM) for a in results))
        return (results[0],) + tuple(jnp.transpose(a, (1, 2, 0)) for a in results[1:])

    tile = P("gx", "gy", "grp")
    in_specs = (
        tile,
        P("gx", "gy"),
        P("gx", "gy"),
        tile,
        tile,
        P(),
        P(),
        P("grp", None),
        P("grp", None),
        P(None, "grp"),
        P(None, "grp"),
    )
    return jax.shard_map(body, mesh=mesh, in_specs=in_specs, out_specs=(tile,) * 5, check_vma=False)
```

```python
import functools

import jax
import jax.numpy as jnp
import numpy as np
from jax import lax
from jax.experimental import pallas as pl
from jax.experimental.pallas import tpu as pltpu
from jax.sharding import PartitionSpec as P

NF = 32
ND = 36
NLEV = 40
WAVE_SECTIONS = 3
NFL = 16
LANES = 128
MESH = pl.DeviceIdType.MESH

highest = lax.Precision.HIGHEST
inter_step = 0.1
ocean_step = 0.4
coriolis = 0.5
viscosity = 0.1


def exact_dot(a, b):
    return jnp.dot(a, b, precision=highest, preferred_element_type=jnp.float32)


def dot_on(a, b, dim_a, dim_b, precision=highest):
    return lax.dot_general(
        a, b, (((dim_a,), (dim_b,)), ((), ())), precision=precision, preferred_element_type=jnp.float32
    )


def sweep(centre, back_one, back_two, next_one, next_two, velocity):
    up = velocity >= 0.0
    one = jnp.where(up, back_one, next_one)
    two = jnp.where(up, back_two, next_two)
    size = jnp.abs(velocity)
    half = 0.5 * size
    return centre - half * (3.0 * centre - 4.0 * one + two) + half * size * (centre - 2.0 * one + two)


def iota(shape, dim):
    return lax.broadcasted_iota(jnp.int32, shape, dim)


class Move:
    def __init__(self, src, dst, send, recv, device, sends, receives):
        self.copy = pltpu.make_async_remote_copy(
            src_ref=src, dst_ref=dst, send_sem=send, recv_sem=recv, device_id=device, device_id_type=MESH
        )
        self.sends, self.receives = sends, receives

    def when(self, cond, act):
        if cond is True:
            act()
        else:
            pl.when(cond)(act)

    def start(self):
        self.when(self.sends, self.copy.start)

    def wait_send(self):
        self.when(self.sends, self.copy.wait_send)

    def wait_recv(self):
        self.when(self.receives, self.copy.wait_recv)


def kernel(
    sizes,
    spectrum_hbm,
    wet_mask,
    ocean_source,
    ocean_u,
    ocean_v,
    angles,
    cw,
    dw,
    left_hbm,
    right_hbm,
    out_hbm,
    mixing,
    spec_out,
    u_out,
    v_out,
    du_out,
    dv_out,
    spectrum,
    left,
    right,
    out_map,
    load_sem,
    pack,
    currents,
    masked,
    packs,
    own_flow,
    flow,
    flow_edge,
    flow_halo,
    field,
    edge,
    halo_x,
    halo_y,
    corner,
    halo_c,
    speed_x,
    speed_y,
    turn,
    speed_l,
    speed_r,
    wide,
    source,
    mix,
    ocean,
    ocean_next,
    row_halo,
    col_edge,
    col_halo,
    drift_q,
    drift_n,
    init_send,
    init_recv,
    wave_send,
    wave_recv,
    sea_send,
    sea_recv,
):
    nx, ny = sizes
    loads = [
        pltpu.make_async_copy(src, dst, load_sem.at[k])
        for k, (src, dst) in enumerate(
            ((spectrum_hbm, spectrum), (left_hbm, left), (right_hbm, right), (out_hbm, out_map))
        )
    ]
    for load in loads:
        load.start()
    tile_x, tile_y, bins = spectrum.shape
    half = tile_y // 2
    own = u_out.shape[0]
    rows = 2 * tile_x
    g, gx, gy = lax.axis_index("grp"), lax.axis_index("gx"), lax.axis_index("gy")
    z, y = gx // 2, gx % 2
    q = 2 * gy + y
    nz, nq = nx // 2, 2 * ny

    def at(dg=0, x=gx, c=gy):
        return {"grp": (g + dg) % 2, "gx": x, "gy": c}

    pair = 2 * z + 1 - y

    def q_at(dz, dq):
        qq = q + dq
        return at(0, 2 * (z + dz) + qq % 2, qq // 2)

    def inside(value, step, limit):
        return value + step >= 0 if step < 0 else value + step < limit

    def both(dz, dq):
        cond = inside(q, dq, nq)
        return cond if dz == 0 else cond & inside(z, dz, nz)

    friends = [(True, at(1)), (True, at(0, pair)), (True, at(1, pair))]
    friends += [(inside(z, d, nz), at(0, gx + 2 * d)) for d in (-1, 1)]
    friends += [(both(dz, dq), q_at(dz, dq)) for dq in (-1, 1) for dz in (-1, 0, 1)]
    friends += [(inside(gx, d, nx), at(0, gx + d)) for d in (-1, 1)]
    friends += [(inside(gy, d, ny), at(0, gx, gy + d)) for d in (-1, 1)]
    barrier = pltpu.get_barrier_semaphore()
    total = 0
    for cond, device in friends:

        def hello(device=device):
            pl.semaphore_signal(barrier, inc=1, device_id=device, device_id_type=MESH)

        if cond is True:
            hello()
            total = total + 1
        else:
            pl.when(cond)(hello)
            total = total + jnp.where(cond, 1, 0)

    columns = tile_x * tile_y

    def as_columns(table):
        ones = jnp.ones((1, LANES), jnp.float32)
        values = table[...].astype(jnp.float32)
        return jnp.concatenate([dot_on(values[r : r + 1], ones, 0, 0) for r in range(tile_x)], axis=0)

    place_i, place_j = iota((own, LANES), 0), iota((own, LANES), 1)
    place_u = jnp.where(place_j == place_i + own * g, 1.0, 0.0)
    place_v = jnp.where(place_j == place_i + own * g + NLEV, 1.0, 0.0)
    for r in range(tile_x):
        pack[r * tile_y : (r + 1) * tile_y] = dot_on(ocean_u[:, r, :], place_u, 0, 0) + dot_on(
            ocean_v[:, r, :], place_v, 0, 0
        )
    pack[columns:] = dot_on(mixing[...], place_u, 0, 0)
    wet_wide = as_columns(wet_mask)
    wet_n = wet_wide[:, 0:1]

    @pl.when(z == 0)
    def _():
        halo_x[:, 0] = jnp.zeros_like(halo_x[:, 0])

    @pl.when(z == nz - 1)
    def _():
        halo_x[:, 1] = jnp.zeros_like(halo_x[:, 1])

    for side, dq in ((0, -1), (1, 1)):

        @pl.when(jnp.logical_not(inside(q, dq, nq)))
        def _():
            halo_y[:, side] = jnp.zeros_like(halo_y[:, side])
            halo_c[:, side] = jnp.zeros_like(halo_c[:, side])
            flow_halo[side] = jnp.zeros_like(flow_halo[side])

        for slot, dz in ((0, -1), (1, 1)):

            @pl.when(inside(q, dq, nq) & jnp.logical_not(inside(z, dz, nz)))
            def _():
                halo_c[:, side, slot] = jnp.zeros_like(halo_c[:, side, slot])

    for side, d in ((0, -1), (1, 1)):

        @pl.when(jnp.logical_not(inside(gx, d, nx)))
        def _():
            row_halo[:, side] = jnp.zeros_like(row_halo[:, side])

        @pl.when(jnp.logical_not(inside(gy, d, ny)))
        def _():
            col_halo[:, side] = jnp.zeros_like(col_halo[:, side])

    loads[0].wait()
    masked[...] = (spectrum[...].reshape(columns, bins) * wet_n).reshape(tile_x, tile_y, bins)

    pl.semaphore_wait(barrier, total)

    to_grp = Move(pack, packs, init_send.at[0], init_recv.at[0], at(1), True, True)
    to_grp.start()
    away = pl.ds(pl.multiple_of(half * (1 - y), 8), half)
    mine = pl.ds(pl.multiple_of(half * y, 8), half)
    my_rows = pl.ds(tile_x * y, tile_x)
    to_pair = [
        Move(
            masked.at[row, away, :],
            field.at[tile_x * y + row],
            init_send.at[k],
            init_recv.at[k],
            at(0, pair),
            True,
            True,
        )
        for k, row in ((1, y), (9, 1 - y))
    ]
    for m in to_pair:
        m.start()
    field[my_rows] = masked[:, mine, :]

    def wave_moves(s):
        moves = []
        for near in (True, False):
            for side, dz in ((0, -1), (1, 1)):
                layer = 0 if near == (dz < 0) else 1
                moves.append(
                    Move(
                        field.at[layer if dz < 0 else rows - 2 + layer],
                        halo_x.at[s, 1 - side, layer],
                        wave_send.at[s, len(moves)],
                        wave_recv.at[s, len(moves)],
                        at(0, gx + 2 * dz),
                        inside(z, dz, nz),
                        inside(z, -dz, nz),
                    )
                )
        k = 4
        for side, dq in ((0, -1), (1, 1)):
            for dz in (-1, 0, 1):
                moves.append(
                    Move(
                        edge.at[s, side] if dz == 0 else corner.at[s, side, (1 + dz) // 2],
                        halo_y.at[s, 1 - side] if dz == 0 else halo_c.at[s, 1 - side, (1 - dz) // 2],
                        wave_send.at[s, k],
                        wave_recv.at[s, k],
                        q_at(dz, dq),
                        both(dz, dq),
                        both(-dz, -dq),
                    )
                )
                k += 1
        return moves

    first_moves = wave_moves(0)
    for k in (0, 2):
        pl.when(y == 0)(first_moves[k].start)
        pl.when(y == 1)(first_moves[k + 1].start)

    chosen_at = as_columns(ocean_source)[:, 0:1]
    chosen = jnp.where(iota((columns, columns), 1).astype(jnp.float32) == chosen_at, 1.0, 0.0)
    currents[...] = jnp.zeros_like(currents)
    currents[0:NF, 0:NLEV] = cw[...]
    currents[NF : 2 * NF] = pltpu.roll(currents[0:NF], NLEV, 1)
    to_grp.wait_recv()
    everything = pack[...] + packs[...]
    ocean[...] = everything[:columns].reshape(ocean.shape)
    mix[...] = jnp.zeros_like(mix)
    mix[0:NLEV] = everything[columns:]
    mix[NLEV : 2 * NLEV] = pltpu.roll(everything[columns:], NLEV, 1)
    felt = exact_dot(chosen, dot_on(everything[:columns], currents[...], 1, 1))
    felt = felt + jnp.where(iota((columns, LANES), 1) == 2 * NF, wet_n, 0.0)
    own_flow[...] = felt.reshape(own_flow.shape)
    flow_pair = Move(
        own_flow.at[:, away, :], flow.at[my_rows], init_send.at[2], init_recv.at[2], at(0, pair), True, True
    )
    flow_pair.start()
    flow[my_rows] = own_flow[:, mine, :]

    def sea_moves(k, array):
        moves = []
        for side, d in ((0, -1), (1, 1)):
            moves.append(
                Move(
                    array.at[0 if d < 0 else tile_x - 1],
                    row_halo.at[k, 1 - side],
                    sea_send.at[k, side],
                    sea_recv.at[k, side],
                    at(0, gx + d),
                    inside(gx, d, nx),
                    inside(gx, -d, nx),
                )
            )
            moves.append(
                Move(
                    col_edge.at[k, side],
                    col_halo.at[k, 1 - side],
                    sea_send.at[k, 2 + side],
                    sea_recv.at[k, 2 + side],
                    at(0, gx, gy + d),
                    inside(gy, d, ny),
                    inside(gy, -d, ny),
                )
            )
        return moves

    def set_col_edges(k, array):
        for side, column in ((0, 0), (1, tile_y - 1)):
            for r in range(tile_x):
                col_edge[k, side, r : r + 1, :] = array[r, column : column + 1, :]

    lane = iota((1, bins), 1)
    frequency = (g * NFL + (lane & (NFL - 1))).astype(jnp.float32)
    group_speed = 0.2 + 0.4 * (NF - 1 - frequency) / (NF - 1)
    turning = 0.5 * (frequency + 1.0) / NF
    cosine, sine = angles[0:1, :], angles[1:2, :]
    spread_i = iota((LANES, bins), 0)
    spread_f = g * NFL + (iota((LANES, bins), 1) & (NFL - 1))
    spread_x = jnp.where(spread_i == spread_f, 1.0, 0.0)
    spread_y = jnp.where(spread_i == spread_f + NF, 1.0, 0.0)

    def set_edges(s):
        for side, first in ((0, 0), (1, half - 2)):
            for r in range(rows):
                pair_of = field[r, first : first + 2, :]
                edge[s, side, 2 * r : 2 * r + 2, :] = pair_of
                corner[s, side, r // 2, 2 * (r % 2) : 2 * (r % 2) + 2, :] = pair_of

    def interaction():
        now = field[...].reshape(rows * half, bins).astype(jnp.bfloat16)
        product = jnp.dot(now, left[...], preferred_element_type=jnp.float32) * jnp.dot(
            now, right[...], preferred_element_type=jnp.float32
        )
        result = dot_on(product.astype(jnp.bfloat16), out_map[...], 1, 1, None)
        source[...] = (inter_step * result).reshape(source.shape)

    def finish(s, moves):
        for m in moves[4:]:
            m.wait_recv()
        for side, speed, start in ((0, speed_l, 6), (1, speed_r, half + 8)):
            here = halo_y[s, side]
            before, after = (jnp.concatenate([halo_c[s, side, i]] * 2, axis=0) for i in range(2))
            low = iota((8, bins), 0)

            def joined(a, b, n):
                return jnp.where(low < n, pltpu.roll(a, n, 0), pltpu.roll(b, n, 0))

            packed = sweep(
                here,
                joined(before, here, 2),
                joined(before, here, 4),
                joined(here, after, 6),
                joined(here, after, 4),
                speed[...],
            )
            for r in range(rows):
                wide[r, start : start + 2, :] = packed[2 * r : 2 * r + 2]

        def line(r):
            if r < 0:
                return halo_x[s, 0, r + 2]
            if r >= rows:
                return halo_x[s, 1, r - rows]
            return field[r]

        waits = {1: moves[0:2], 0: moves[2:4]}
        for r in [*range(1, rows - 1), 0, rows - 1]:
            for m in waits.get(r, ()):
                m.wait_recv()
            wide[r, 8 : 8 + half, :] = sweep(
                line(r), line(r - 1), line(r - 2), line(r + 1), line(r + 2), speed_x[r]
            )
            b = sweep(
                wide[r, 8 : 8 + half, :],
                wide[r, 7 : 7 + half, :],
                wide[r, 6 : 6 + half, :],
                wide[r, 9 : 9 + half, :],
                wide[r, 10 : 10 + half, :],
                speed_y[r],
            )
            t = turn[r]
            behind = jnp.concatenate([b[:, bins - NFL :], b[:, : bins - NFL]], axis=1)
            ahead = jnp.concatenate([b[:, NFL:], b[:, :NFL]], axis=1)
            c = b - jnp.abs(t) * (b - jnp.where(t >= 0.0, behind, ahead))
            source[r] = flow[r, :, 2 * NF : 2 * NF + 1] * (c + source[r])
        for m in moves:
            m.wait_send()
        field[...] = source[...]

    def flow_moves():
        return [
            Move(
                flow_edge.at[side],
                flow_halo.at[1 - side],
                init_send.at[3 + side],
                init_recv.at[3 + side],
                q_at(0, dq),
                inside(q, dq, nq),
                inside(q, -dq, nq),
            )
            for side, dq in ((0, -1), (1, 1))
        ]

    def received(k, row):
        Move(
            masked.at[row, away, :], field.at[tile_x * (1 - y) + row], init_send.at[k], init_recv.at[k], at(0, pair), True, True
        ).wait_recv()

    received(1, 1 - y)
    pl.when(y == 1)(first_moves[0].start)
    pl.when(y == 0)(first_moves[1].start)
    received(9, y)
    set_edges(0)
    for m in first_moves[4:]:
        m.start()
    pl.when(y == 1)(first_moves[2].start)
    pl.when(y == 0)(first_moves[3].start)
    set_col_edges(0, ocean)
    flow_pair.wait_recv()
    for side, first in ((0, 0), (1, half - 2)):
        for r in range(rows):
            flow_edge[side, 2 * r : 2 * r + 2, :] = flow[r, first : first + 2, :]
    edges_flow = flow_moves()
    for m in edges_flow:
        m.start()
    sea_first = sea_moves(0, ocean)
    for m in sea_first:
        m.start()
    fq = flow[...].reshape(rows * half, LANES)
    fx = exact_dot(fq, spread_x)
    fy = exact_dot(fq, spread_y)
    speed_x[...] = (group_speed * cosine + fx).reshape(speed_x.shape)
    speed_y[...] = (group_speed * sine + fy).reshape(speed_x.shape)
    turn[...] = (turning * (sine * fx - cosine * fy)).reshape(speed_x.shape)
    for load in loads[1:]:
        load.wait()
    interaction()
    for m in edges_flow:
        m.wait_recv()
    speed_l[...] = group_speed * cosine + exact_dot(flow_halo[0], spread_x)
    speed_r[...] = group_speed * cosine + exact_dot(flow_halo[1], spread_x)
    finish(0, first_moves)

    def section(s, carry):
        set_edges(s)
        moves = wave_moves(s)
        for m in moves[4:] + moves[:4]:
            m.start()
        interaction()
        finish(s, moves)
        return carry

    lax.fori_loop(1, WAVE_SECTIONS, section, 0)

    their_rows = pl.ds(tile_x * (1 - y), tile_x)
    back = Move(
        field.at[their_rows], spec_out.at[:, mine, :], init_send.at[5], init_recv.at[5], at(0, pair), True, True
    )
    depth = dot_on(dw[...], spread_x[0:NF], 0, 0)
    unused = jnp.zeros((LANES - 2 * NLEV, bins), jnp.float32)
    profile = jnp.concatenate([depth * cosine, depth * sine, unused], axis=0)
    drift = lax.dot_general(
        field[...].reshape(rows * half, bins),
        profile,
        (((1,), (1,)), ((), ())),
        precision=highest,
        preferred_element_type=jnp.float32,
    )
    drift_q[...] = drift.reshape(drift_q.shape)
    drift_moves = [
        Move(
            drift_q.at[pl.ds(tile_x * yy, tile_x)],
            drift_n.at[g, :, mine, :],
            init_send.at[6 + k],
            init_recv.at[6 + k],
            device,
            True,
            True,
        )
        for k, (yy, device) in enumerate(((y, at(1)), (1 - y, at(1, pair)), (1 - y, at(0, pair))))
    ]
    for m in drift_moves:
        m.start()
    back.start()
    spec_out[:, mine, :] = field[my_rows]
    drift_n[g, :, mine, :] = drift_q[my_rows]

    lane_n = iota((columns, LANES), 1)
    column_n = iota((tile_y, LANES), 0)

    def neighbours(k, array):
        result = []
        for r in range(tile_x):
            a = array[r]
            below = array[r - 1] if r > 0 else row_halo[k, 0]
            above = array[r + 1] if r < tile_x - 1 else row_halo[k, 1]
            lower = jnp.where(column_n == 0, col_halo[k, 0, r : r + 1, :], pltpu.roll(a, 1, 0))
            upper = jnp.where(column_n == tile_y - 1, col_halo[k, 1, r : r + 1, :], pltpu.roll(a, tile_y - 1, 0))
            result.append(above + below + upper + lower - 4.0 * a)
        return jnp.concatenate(result, axis=0)

    def swapped(a):
        from_v = pltpu.roll(a, LANES - NLEV, 1)
        from_u = pltpu.roll(a, NLEV, 1)
        return jnp.where(lane_n < NLEV, from_v, jnp.where(lane_n < 2 * NLEV, -from_u, 0.0))

    def ocean_section(array, laplace, drift_all):
        flat = array[...].reshape(columns, LANES)
        first = flat + ocean_step * (coriolis * swapped(flat + drift_all) + viscosity * laplace)
        return wet_n * (first + exact_dot(first, mix[...]))

    for m in sea_first:
        m.wait_recv()
    laplace_first = neighbours(0, ocean)
    for k, device in enumerate((at(1), at(1, pair), at(0, pair))):
        landing = drift_n.at[1 - g if k < 2 else g, :, mine if k == 0 else away, :]
        Move(drift_q.at[my_rows], landing, init_send.at[6 + k], init_recv.at[6 + k], device, True, True).wait_recv()
    drift_all = (drift_n[0] + drift_n[1]).reshape(columns, LANES)
    ocean_next[...] = ocean_section(ocean, laplace_first, drift_all).reshape(ocean.shape)
    set_col_edges(1, ocean_next)
    sea_second = sea_moves(1, ocean_next)
    for m in sea_second:
        m.start()

    def picking(offset):
        i, j = iota((LANES, own), 0), iota((LANES, own), 1)
        return jnp.where(i == j + own * g + offset, 1.0, 0.0)

    pick_u, pick_v = picking(0), picking(NLEV)

    def give(out, pick, values):
        for r in range(tile_x):
            out[:, r, :] = dot_on(pick, values[r * tile_y : (r + 1) * tile_y], 0, 1)

    give(du_out, pick_u, drift_all)
    give(dv_out, pick_v, drift_all)
    for m in sea_second:
        m.wait_recv()
    final = ocean_section(ocean_next, neighbours(1, ocean_next), drift_all)
    give(u_out, pick_u, final)
    give(v_out, pick_v, final)
    back.wait_recv()
    for m in [to_grp, flow_pair, back] + to_pair + edges_flow + drift_moves + sea_first + sea_second:
        m.wait_send()


def store_kernel(*refs):
    count = (len(refs) - 1) // 2
    copies = [pltpu.make_async_copy(refs[i], refs[count + i], refs[-1].at[i]) for i in range(count)]
    for copy in copies:
        copy.start()
    for copy in copies:
        copy.wait()


def solution(mesh):
    sizes = (mesh.shape["gx"], mesh.shape["gy"])
    theta = 2.0 * np.pi * np.arange(ND) / ND
    table = np.zeros((8, ND * NFL), np.float32)
    table[0] = np.repeat(np.cos(theta), NFL)
    table[1] = np.repeat(np.sin(theta), NFL)

    def body(spectrum, wet_mask, ocean_source, ocean_u, ocean_v, current_weights, drift_weights, inter_left, inter_right, inter_out, mixing):
        tile_x, tile_y, bins = spectrum.shape
        half, rows = tile_y // 2, 2 * tile_x
        own = ocean_u.shape[2]
        columns = tile_x * tile_y
        f32 = jnp.float32
        vmem = pl.BlockSpec(memory_space=pltpu.VMEM)
        sea = (tile_x, tile_y, LANES)
        sections = WAVE_SECTIONS
        wave = (rows, half, bins)

        def V(*shape):
            return pltpu.VMEM(shape, f32)

        def D(*shape):
            return pltpu.SemaphoreType.DMA(shape)

        outs = (jax.ShapeDtypeStruct(spectrum.shape, f32),) + (
            jax.ShapeDtypeStruct((own, tile_x, tile_y), f32),
        ) * 4
        anywhere = pl.BlockSpec(memory_space=pl.ANY)
        results = pl.pallas_call(
            functools.partial(kernel, sizes),
            out_shape=tuple(pltpu.VMEM(a.shape, a.dtype) for a in outs),
            in_specs=[anywhere] + [vmem] * 7 + [anywhere] * 3 + [vmem],
            out_specs=(vmem,) * 5,
            scratch_shapes=[
                V(tile_x, tile_y, bins),
                pltpu.VMEM(inter_left.shape, inter_left.dtype),
                pltpu.VMEM(inter_right.shape, inter_right.dtype),
                pltpu.VMEM(inter_out.shape[::-1], inter_out.dtype),
                D(4),
                V(columns + NLEV, LANES),
                V(LANES, LANES),
                V(tile_x, tile_y, bins),
                V(columns + NLEV, LANES),
                V(*sea),
                V(rows, half, LANES),
                V(2, 8, LANES),
                V(2, 8, LANES),
                V(*wave),
                V(sections, 2, 8, bins),
                V(sections, 2, 2, half, bins),
                V(sections, 2, 8, bins),
                V(sections, 2, 2, 4, bins),
                V(sections, 2, 2, 4, bins),
                V(*wave),
                V(*wave),
                V(*wave),
                V(8, bins),
                V(8, bins),
                V(rows, half + 16, bins),
                V(*wave),
                V(LANES, LANES),
                V(*sea),
                V(*sea),
                V(2, 2, tile_y, LANES),
                V(2, 2, 8, LANES),
                V(2, 2, 8, LANES),
                V(rows, half, LANES),
                V(2, *sea),
                D(10),
                D(10),
                D(sections, 10),
                D(sections, 10),
                D(2, 4),
                D(2, 4),
            ],
            compiler_params=pltpu.CompilerParams(collective_id=0, has_side_effects=True),
        )(
            spectrum,
            wet_mask,
            ocean_source,
            jnp.transpose(ocean_u, (2, 0, 1)),
            jnp.transpose(ocean_v, (2, 0, 1)),
            jnp.asarray(table),
            current_weights.T,
            drift_weights.T,
            inter_left,
            inter_right,
            inter_out.T,
            mixing.T,
        )
        results = pl.pallas_call(
            store_kernel,
            out_shape=outs,
            in_specs=[anywhere] * 5,
            out_specs=(anywhere,) * 5,
            scratch_shapes=[D(5)],
        )(*(pltpu.with_memory_space_constraint(a, pltpu.VMEM) for a in results))
        return (results[0],) + tuple(jnp.transpose(a, (1, 2, 0)) for a in results[1:])

    tile = P("gx", "gy", "grp")
    in_specs = (
        tile,
        P("gx", "gy"),
        P("gx", "gy"),
        tile,
        tile,
        P(),
        P(),
        P("grp", None),
        P("grp", None),
        P(None, "grp"),
        P(None, "grp"),
    )
    return jax.shard_map(body, mesh=mesh, in_specs=in_specs, out_specs=(tile,) * 5, check_vma=False)
```

```python
import functools

import jax
import jax.numpy as jnp
import numpy as np
from jax import lax
from jax.experimental import pallas as pl
from jax.experimental.pallas import tpu as pltpu
from jax.sharding import PartitionSpec as P

NF = 32
ND = 36
NLEV = 40
WAVE_SECTIONS = 3
NFL = 16
LANES = 128
MESH = pl.DeviceIdType.MESH

highest = lax.Precision.HIGHEST
inter_step = 0.1
ocean_step = 0.4
coriolis = 0.5
viscosity = 0.1


def exact_dot(a, b):
    return jnp.dot(a, b, precision=highest, preferred_element_type=jnp.float32)


def dot_on(a, b, dim_a, dim_b, precision=highest):
    return lax.dot_general(
        a, b, (((dim_a,), (dim_b,)), ((), ())), precision=precision, preferred_element_type=jnp.float32
    )


def sweep(centre, back_one, back_two, next_one, next_two, velocity):
    up = velocity >= 0.0
    one = jnp.where(up, back_one, next_one)
    two = jnp.where(up, back_two, next_two)
    size = jnp.abs(velocity)
    half = 0.5 * size
    return centre - half * (3.0 * centre - 4.0 * one + two) + half * size * (centre - 2.0 * one + two)


def iota(shape, dim):
    return lax.broadcasted_iota(jnp.int32, shape, dim)


class Move:
    def __init__(self, src, dst, send, recv, device, sends, receives):
        self.copy = pltpu.make_async_remote_copy(
            src_ref=src, dst_ref=dst, send_sem=send, recv_sem=recv, device_id=device, device_id_type=MESH
        )
        self.sends, self.receives = sends, receives

    def when(self, cond, act):
        if cond is True:
            act()
        else:
            pl.when(cond)(act)

    def start(self):
        self.when(self.sends, self.copy.start)

    def wait_send(self):
        self.when(self.sends, self.copy.wait_send)

    def wait_recv(self):
        self.when(self.receives, self.copy.wait_recv)


def kernel(
    sizes,
    spectrum_hbm,
    wet_mask,
    ocean_source,
    ocean_u,
    ocean_v,
    angles,
    cw,
    dw,
    left_hbm,
    right_hbm,
    out_hbm,
    mixing,
    spec_out,
    u_out,
    v_out,
    du_out,
    dv_out,
    spectrum,
    left,
    right,
    out_map,
    load_sem,
    pack,
    currents,
    profile,
    masked,
    packs,
    own_flow,
    flow,
    flow_edge,
    flow_halo,
    field,
    edge,
    halo_x,
    halo_y,
    corner,
    halo_c,
    speed_x,
    speed_y,
    turn,
    speed_l,
    speed_r,
    wide,
    source,
    mix,
    ocean,
    ocean_next,
    row_halo,
    col_edge,
    col_halo,
    drift_q,
    drift_n,
    init_send,
    init_recv,
    wave_send,
    wave_recv,
    sea_send,
    sea_recv,
):
    nx, ny = sizes
    loads = [
        pltpu.make_async_copy(src, dst, load_sem.at[k])
        for k, (src, dst) in enumerate(
            ((spectrum_hbm, spectrum), (left_hbm, left), (right_hbm, right), (out_hbm, out_map))
        )
    ]
    for load in loads:
        load.start()
    tile_x, tile_y, bins = spectrum.shape
    half = tile_y // 2
    own = u_out.shape[0]
    rows = 2 * tile_x
    g, gx, gy = lax.axis_index("grp"), lax.axis_index("gx"), lax.axis_index("gy")
    z, y = gx // 2, gx % 2
    q = 2 * gy + y
    nz, nq = nx // 2, 2 * ny

    def at(dg=0, x=gx, c=gy):
        return {"grp": (g + dg) % 2, "gx": x, "gy": c}

    pair = 2 * z + 1 - y

    def q_at(dz, dq):
        qq = q + dq
        return at(0, 2 * (z + dz) + qq % 2, qq // 2)

    def inside(value, step, limit):
        return value + step >= 0 if step < 0 else value + step < limit

    def both(dz, dq):
        cond = inside(q, dq, nq)
        return cond if dz == 0 else cond & inside(z, dz, nz)

    friends = [(True, at(1)), (True, at(0, pair)), (True, at(1, pair))]
    friends += [(inside(z, d, nz), at(0, gx + 2 * d)) for d in (-1, 1)]
    friends += [(both(dz, dq), q_at(dz, dq)) for dq in (-1, 1) for dz in (-1, 0, 1)]
    friends += [(inside(gx, d, nx), at(0, gx + d)) for d in (-1, 1)]
    friends += [(inside(gy, d, ny), at(0, gx, gy + d)) for d in (-1, 1)]
    barrier = pltpu.get_barrier_semaphore()
    total = 0
    for cond, device in friends:

        def hello(device=device):
            pl.semaphore_signal(barrier, inc=1, device_id=device, device_id_type=MESH)

        if cond is True:
            hello()
            total = total + 1
        else:
            pl.when(cond)(hello)
            total = total + jnp.where(cond, 1, 0)

    columns = tile_x * tile_y

    def as_columns(table):
        ones = jnp.ones((1, LANES), jnp.float32)
        values = table[...].astype(jnp.float32)
        return jnp.concatenate([dot_on(values[r : r + 1], ones, 0, 0) for r in range(tile_x)], axis=0)

    place_i, place_j = iota((own, LANES), 0), iota((own, LANES), 1)
    place_u = jnp.where(place_j == place_i + own * g, 1.0, 0.0)
    place_v = jnp.where(place_j == place_i + own * g + NLEV, 1.0, 0.0)
    for r in range(tile_x):
        pack[r * tile_y : (r + 1) * tile_y] = dot_on(ocean_u[:, r, :], place_u, 0, 0) + dot_on(
            ocean_v[:, r, :], place_v, 0, 0
        )
    pack[columns:] = dot_on(mixing[...], place_u, 0, 0)
    wet_wide = as_columns(wet_mask)
    wet_n = wet_wide[:, 0:1]

    @pl.when(z == 0)
    def _():
        halo_x[:, 0] = jnp.zeros_like(halo_x[:, 0])

    @pl.when(z == nz - 1)
    def _():
        halo_x[:, 1] = jnp.zeros_like(halo_x[:, 1])

    for side, dq in ((0, -1), (1, 1)):

        @pl.when(jnp.logical_not(inside(q, dq, nq)))
        def _():
            halo_y[:, side] = jnp.zeros_like(halo_y[:, side])
            halo_c[:, side] = jnp.zeros_like(halo_c[:, side])
            flow_halo[side] = jnp.zeros_like(flow_halo[side])

        for slot, dz in ((0, -1), (1, 1)):

            @pl.when(inside(q, dq, nq) & jnp.logical_not(inside(z, dz, nz)))
            def _():
                halo_c[:, side, slot] = jnp.zeros_like(halo_c[:, side, slot])

    for side, d in ((0, -1), (1, 1)):

        @pl.when(jnp.logical_not(inside(gx, d, nx)))
        def _():
            row_halo[:, side] = jnp.zeros_like(row_halo[:, side])

        @pl.when(jnp.logical_not(inside(gy, d, ny)))
        def _():
            col_halo[:, side] = jnp.zeros_like(col_halo[:, side])

    loads[0].wait()
    masked[...] = (spectrum[...].reshape(columns, bins) * wet_n).reshape(tile_x, tile_y, bins)

    pl.semaphore_wait(barrier, total)

    to_grp = Move(pack, packs, init_send.at[0], init_recv.at[0], at(1), True, True)
    to_grp.start()
    away = pl.ds(pl.multiple_of(half * (1 - y), 8), half)
    mine = pl.ds(pl.multiple_of(half * y, 8), half)
    my_rows = pl.ds(tile_x * y, tile_x)
    to_pair = [
        Move(
            masked.at[row, away, :],
            field.at[tile_x * y + row],
            init_send.at[k],
            init_recv.at[k],
            at(0, pair),
            True,
            True,
        )
        for k, row in ((1, y), (9, 1 - y))
    ]
    for m in to_pair:
        m.start()
    field[my_rows] = masked[:, mine, :]

    def wave_moves(s):
        moves = []
        for near in (True, False):
            for side, dz in ((0, -1), (1, 1)):
                layer = 0 if near == (dz < 0) else 1
                moves.append(
                    Move(
                        field.at[layer if dz < 0 else rows - 2 + layer],
                        halo_x.at[s, 1 - side, layer],
                        wave_send.at[s, len(moves)],
                        wave_recv.at[s, len(moves)],
                        at(0, gx + 2 * dz),
                        inside(z, dz, nz),
                        inside(z, -dz, nz),
                    )
                )
        k = 4
        for side, dq in ((0, -1), (1, 1)):
            for dz in (-1, 0, 1):
                moves.append(
                    Move(
                        edge.at[s, side] if dz == 0 else corner.at[s, side, (1 + dz) // 2],
                        halo_y.at[s, 1 - side] if dz == 0 else halo_c.at[s, 1 - side, (1 - dz) // 2],
                        wave_send.at[s, k],
                        wave_recv.at[s, k],
                        q_at(dz, dq),
                        both(dz, dq),
                        both(-dz, -dq),
                    )
                )
                k += 1
        return moves

    first_moves = wave_moves(0)
    for k in (0, 2):
        pl.when(y == 0)(first_moves[k].start)
        pl.when(y == 1)(first_moves[k + 1].start)

    chosen_at = as_columns(ocean_source)[:, 0:1]
    chosen = jnp.where(iota((columns, columns), 1).astype(jnp.float32) == chosen_at, 1.0, 0.0)
    currents[...] = jnp.zeros_like(currents)
    currents[0:NF, 0:NLEV] = cw[...]
    currents[NF : 2 * NF] = pltpu.roll(currents[0:NF], NLEV, 1)
    to_grp.wait_recv()
    everything = pack[...] + packs[...]
    ocean[...] = everything[:columns].reshape(ocean.shape)
    mix[...] = jnp.zeros_like(mix)
    mix[0:NLEV] = everything[columns:]
    mix[NLEV : 2 * NLEV] = pltpu.roll(everything[columns:], NLEV, 1)
    felt = exact_dot(chosen, dot_on(everything[:columns], currents[...], 1, 1))
    felt = felt + jnp.where(iota((columns, LANES), 1) == 2 * NF, wet_n, 0.0)
    own_flow[...] = felt.reshape(own_flow.shape)
    flow_pair = Move(
        own_flow.at[:, away, :], flow.at[my_rows], init_send.at[2], init_recv.at[2], at(0, pair), True, True
    )
    flow_pair.start()
    flow[my_rows] = own_flow[:, mine, :]

    def sea_moves(k, array):
        moves = []
        for side, d in ((0, -1), (1, 1)):
            moves.append(
                Move(
                    array.at[0 if d < 0 else tile_x - 1],
                    row_halo.at[k, 1 - side],
                    sea_send.at[k, side],
                    sea_recv.at[k, side],
                    at(0, gx + d),
                    inside(gx, d, nx),
                    inside(gx, -d, nx),
                )
            )
            moves.append(
                Move(
                    col_edge.at[k, side],
                    col_halo.at[k, 1 - side],
                    sea_send.at[k, 2 + side],
                    sea_recv.at[k, 2 + side],
                    at(0, gx, gy + d),
                    inside(gy, d, ny),
                    inside(gy, -d, ny),
                )
            )
        return moves

    def set_col_edges(k, array):
        for side, column in ((0, 0), (1, tile_y - 1)):
            for r in range(tile_x):
                col_edge[k, side, r : r + 1, :] = array[r, column : column + 1, :]

    lane = iota((1, bins), 1)
    frequency = (g * NFL + (lane & (NFL - 1))).astype(jnp.float32)
    group_speed = 0.2 + 0.4 * (NF - 1 - frequency) / (NF - 1)
    turning = 0.5 * (frequency + 1.0) / NF
    cosine, sine = angles[0:1, :], angles[1:2, :]
    spread_i = iota((LANES, bins), 0)
    spread_f = g * NFL + (iota((LANES, bins), 1) & (NFL - 1))
    spread_x = jnp.where(spread_i == spread_f, 1.0, 0.0)
    spread_y = jnp.where(spread_i == spread_f + NF, 1.0, 0.0)

    def set_edges(s):
        for side, first in ((0, 0), (1, half - 2)):
            for r in range(rows):
                pair_of = field[r, first : first + 2, :]
                edge[s, side, 2 * r : 2 * r + 2, :] = pair_of
                corner[s, side, r // 2, 2 * (r % 2) : 2 * (r % 2) + 2, :] = pair_of

    def interaction():
        now = field[...].reshape(rows * half, bins).astype(jnp.bfloat16)
        product = jnp.dot(now, left[...], preferred_element_type=jnp.float32) * jnp.dot(
            now, right[...], preferred_element_type=jnp.float32
        )
        result = dot_on(product.astype(jnp.bfloat16), out_map[...], 1, 1, None)
        source[...] = (inter_step * result).reshape(source.shape)

    def finish(s, moves):
        for m in moves[4:]:
            m.wait_recv()
        for side, speed, start in ((0, speed_l, 6), (1, speed_r, half + 8)):
            here = halo_y[s, side]
            before, after = (jnp.concatenate([halo_c[s, side, i]] * 2, axis=0) for i in range(2))
            low = iota((8, bins), 0)

            def joined(a, b, n):
                return jnp.where(low < n, pltpu.roll(a, n, 0), pltpu.roll(b, n, 0))

            packed = sweep(
                here,
                joined(before, here, 2),
                joined(before, here, 4),
                joined(here, after, 6),
                joined(here, after, 4),
                speed[...],
            )
            for r in range(rows):
                wide[r, start : start + 2, :] = packed[2 * r : 2 * r + 2]

        def line(r):
            if r < 0:
                return halo_x[s, 0, r + 2]
            if r >= rows:
                return halo_x[s, 1, r - rows]
            return field[r]

        waits = {1: moves[0:2], 0: moves[2:4]}
        for r in [*range(1, rows - 1), 0, rows - 1]:
            for m in waits.get(r, ()):
                m.wait_recv()
            wide[r, 8 : 8 + half, :] = sweep(
                line(r), line(r - 1), line(r - 2), line(r + 1), line(r + 2), speed_x[r]
            )
            b = sweep(
                wide[r, 8 : 8 + half, :],
                wide[r, 7 : 7 + half, :],
                wide[r, 6 : 6 + half, :],
                wide[r, 9 : 9 + half, :],
                wide[r, 10 : 10 + half, :],
                speed_y[r],
            )
            t = turn[r]
            behind = jnp.concatenate([b[:, bins - NFL :], b[:, : bins - NFL]], axis=1)
            ahead = jnp.concatenate([b[:, NFL:], b[:, :NFL]], axis=1)
            c = b - jnp.abs(t) * (b - jnp.where(t >= 0.0, behind, ahead))
            source[r] = flow[r, :, 2 * NF : 2 * NF + 1] * (c + source[r])
        for m in moves:
            m.wait_send()
        field[...] = source[...]

    def flow_moves():
        return [
            Move(
                flow_edge.at[side],
                flow_halo.at[1 - side],
                init_send.at[3 + side],
                init_recv.at[3 + side],
                q_at(0, dq),
                inside(q, dq, nq),
                inside(q, -dq, nq),
            )
            for side, dq in ((0, -1), (1, 1))
        ]

    def received(k, row):
        Move(
            masked.at[row, away, :], field.at[tile_x * (1 - y) + row], init_send.at[k], init_recv.at[k], at(0, pair), True, True
        ).wait_recv()

    received(1, 1 - y)
    pl.when(y == 1)(first_moves[0].start)
    pl.when(y == 0)(first_moves[1].start)
    received(9, y)
    set_edges(0)
    for m in first_moves[4:]:
        m.start()
    pl.when(y == 1)(first_moves[2].start)
    pl.when(y == 0)(first_moves[3].start)
    set_col_edges(0, ocean)
    flow_pair.wait_recv()
    for side, first in ((0, 0), (1, half - 2)):
        for r in range(rows):
            flow_edge[side, 2 * r : 2 * r + 2, :] = flow[r, first : first + 2, :]
    edges_flow = flow_moves()
    for m in edges_flow:
        m.start()
    sea_first = sea_moves(0, ocean)
    for m in sea_first:
        m.start()
    fq = flow[...].reshape(rows * half, LANES)
    fx = exact_dot(fq, spread_x)
    fy = exact_dot(fq, spread_y)
    speed_x[...] = (group_speed * cosine + fx).reshape(speed_x.shape)
    speed_y[...] = (group_speed * sine + fy).reshape(speed_x.shape)
    turn[...] = (turning * (sine * fx - cosine * fy)).reshape(speed_x.shape)
    for load in loads[1:]:
        load.wait()
    interaction()
    depth = dot_on(dw[...], spread_x[0:NF], 0, 0)
    profile[0:NLEV] = depth * cosine
    profile[NLEV : 2 * NLEV] = depth * sine
    profile[2 * NLEV :] = jnp.zeros((LANES - 2 * NLEV, bins), jnp.float32)
    for m in edges_flow:
        m.wait_recv()
    speed_l[...] = group_speed * cosine + exact_dot(flow_halo[0], spread_x)
    speed_r[...] = group_speed * cosine + exact_dot(flow_halo[1], spread_x)
    finish(0, first_moves)

    def section(s, carry):
        set_edges(s)
        moves = wave_moves(s)
        for m in moves[4:] + moves[:4]:
            m.start()
        interaction()
        finish(s, moves)
        return carry

    lax.fori_loop(1, WAVE_SECTIONS, section, 0)

    their_rows = pl.ds(tile_x * (1 - y), tile_x)
    back = Move(
        field.at[their_rows], spec_out.at[:, mine, :], init_send.at[5], init_recv.at[5], at(0, pair), True, True
    )
    drift = lax.dot_general(
        field[...].reshape(rows * half, bins),
        profile[...],
        (((1,), (1,)), ((), ())),
        precision=highest,
        preferred_element_type=jnp.float32,
    )
    drift_q[...] = drift.reshape(drift_q.shape)
    drift_moves = [
        Move(
            drift_q.at[pl.ds(tile_x * yy, tile_x)],
            drift_n.at[g, :, mine, :],
            init_send.at[6 + k],
            init_recv.at[6 + k],
            device,
            True,
            True,
        )
        for k, (yy, device) in enumerate(((y, at(1)), (1 - y, at(1, pair)), (1 - y, at(0, pair))))
    ]
    for k in (1, 2, 0):
        drift_moves[k].start()
    back.start()
    spec_out[:, mine, :] = field[my_rows]
    drift_n[g, :, mine, :] = drift_q[my_rows]

    lane_n = iota((columns, LANES), 1)
    column_n = iota((tile_y, LANES), 0)

    def neighbours(k, array):
        result = []
        for r in range(tile_x):
            a = array[r]
            below = array[r - 1] if r > 0 else row_halo[k, 0]
            above = array[r + 1] if r < tile_x - 1 else row_halo[k, 1]
            lower = jnp.where(column_n == 0, col_halo[k, 0, r : r + 1, :], pltpu.roll(a, 1, 0))
            upper = jnp.where(column_n == tile_y - 1, col_halo[k, 1, r : r + 1, :], pltpu.roll(a, tile_y - 1, 0))
            result.append(above + below + upper + lower - 4.0 * a)
        return jnp.concatenate(result, axis=0)

    def swapped(a):
        from_v = pltpu.roll(a, LANES - NLEV, 1)
        from_u = pltpu.roll(a, NLEV, 1)
        return jnp.where(lane_n < NLEV, from_v, jnp.where(lane_n < 2 * NLEV, -from_u, 0.0))

    def ocean_section(array, laplace, drift_all):
        flat = array[...].reshape(columns, LANES)
        first = flat + ocean_step * (coriolis * swapped(flat + drift_all) + viscosity * laplace)
        return wet_n * (first + exact_dot(first, mix[...]))

    for m in sea_first:
        m.wait_recv()
    laplace_first = neighbours(0, ocean)
    for k, device in enumerate((at(1), at(1, pair), at(0, pair))):
        landing = drift_n.at[1 - g if k < 2 else g, :, mine if k == 0 else away, :]
        Move(drift_q.at[my_rows], landing, init_send.at[6 + k], init_recv.at[6 + k], device, True, True).wait_recv()
    drift_all = (drift_n[0] + drift_n[1]).reshape(columns, LANES)
    ocean_next[...] = ocean_section(ocean, laplace_first, drift_all).reshape(ocean.shape)
    set_col_edges(1, ocean_next)
    sea_second = sea_moves(1, ocean_next)
    for m in sea_second:
        m.start()

    def picking(offset):
        i, j = iota((LANES, own), 0), iota((LANES, own), 1)
        return jnp.where(i == j + own * g + offset, 1.0, 0.0)

    pick_u, pick_v = picking(0), picking(NLEV)

    def give(out, pick, values):
        for r in range(tile_x):
            out[:, r, :] = dot_on(pick, values[r * tile_y : (r + 1) * tile_y], 0, 1)

    give(du_out, pick_u, drift_all)
    give(dv_out, pick_v, drift_all)
    for m in sea_second:
        m.wait_recv()
    final = ocean_section(ocean_next, neighbours(1, ocean_next), drift_all)
    give(u_out, pick_u, final)
    give(v_out, pick_v, final)
    back.wait_recv()
    for m in [to_grp, flow_pair, back] + to_pair + edges_flow + drift_moves + sea_first + sea_second:
        m.wait_send()


def store_kernel(*refs):
    count = (len(refs) - 1) // 2
    copies = [pltpu.make_async_copy(refs[i], refs[count + i], refs[-1].at[i]) for i in range(count)]
    for copy in copies:
        copy.start()
    for copy in copies:
        copy.wait()


def solution(mesh):
    sizes = (mesh.shape["gx"], mesh.shape["gy"])
    theta = 2.0 * np.pi * np.arange(ND) / ND
    table = np.zeros((8, ND * NFL), np.float32)
    table[0] = np.repeat(np.cos(theta), NFL)
    table[1] = np.repeat(np.sin(theta), NFL)

    def body(spectrum, wet_mask, ocean_source, ocean_u, ocean_v, current_weights, drift_weights, inter_left, inter_right, inter_out, mixing):
        tile_x, tile_y, bins = spectrum.shape
        half, rows = tile_y // 2, 2 * tile_x
        own = ocean_u.shape[2]
        columns = tile_x * tile_y
        f32 = jnp.float32
        vmem = pl.BlockSpec(memory_space=pltpu.VMEM)
        sea = (tile_x, tile_y, LANES)
        sections = WAVE_SECTIONS
        wave = (rows, half, bins)

        def V(*shape):
            return pltpu.VMEM(shape, f32)

        def D(*shape):
            return pltpu.SemaphoreType.DMA(shape)

        outs = (jax.ShapeDtypeStruct(spectrum.shape, f32),) + (
            jax.ShapeDtypeStruct((own, tile_x, tile_y), f32),
        ) * 4
        anywhere = pl.BlockSpec(memory_space=pl.ANY)
        results = pl.pallas_call(
            functools.partial(kernel, sizes),
            out_shape=tuple(pltpu.VMEM(a.shape, a.dtype) for a in outs),
            in_specs=[anywhere] + [vmem] * 7 + [anywhere] * 3 + [vmem],
            out_specs=(vmem,) * 5,
            scratch_shapes=[
                V(tile_x, tile_y, bins),
                pltpu.VMEM(inter_left.shape, inter_left.dtype),
                pltpu.VMEM(inter_right.shape, inter_right.dtype),
                pltpu.VMEM(inter_out.shape[::-1], inter_out.dtype),
                D(4),
                V(columns + NLEV, LANES),
                V(LANES, LANES),
                V(LANES, bins),
                V(tile_x, tile_y, bins),
                V(columns + NLEV, LANES),
                V(*sea),
                V(rows, half, LANES),
                V(2, 8, LANES),
                V(2, 8, LANES),
                V(*wave),
                V(sections, 2, 8, bins),
                V(sections, 2, 2, half, bins),
                V(sections, 2, 8, bins),
                V(sections, 2, 2, 4, bins),
                V(sections, 2, 2, 4, bins),
                V(*wave),
                V(*wave),
                V(*wave),
                V(8, bins),
                V(8, bins),
                V(rows, half + 16, bins),
                V(*wave),
                V(LANES, LANES),
                V(*sea),
                V(*sea),
                V(2, 2, tile_y, LANES),
                V(2, 2, 8, LANES),
                V(2, 2, 8, LANES),
                V(rows, half, LANES),
                V(2, *sea),
                D(10),
                D(10),
                D(sections, 10),
                D(sections, 10),
                D(2, 4),
                D(2, 4),
            ],
            compiler_params=pltpu.CompilerParams(collective_id=0, has_side_effects=True),
        )(
            spectrum,
            wet_mask,
            ocean_source,
            jnp.transpose(ocean_u, (2, 0, 1)),
            jnp.transpose(ocean_v, (2, 0, 1)),
            jnp.asarray(table),
            current_weights.T,
            drift_weights.T,
            inter_left,
            inter_right,
            inter_out.T,
            mixing.T,
        )
        results = pl.pallas_call(
            store_kernel,
            out_shape=outs,
            in_specs=[anywhere] * 5,
            out_specs=(anywhere,) * 5,
            scratch_shapes=[D(5)],
        )(*(pltpu.with_memory_space_constraint(a, pltpu.VMEM) for a in results))
        return (results[0],) + tuple(jnp.transpose(a, (1, 2, 0)) for a in results[1:])

    tile = P("gx", "gy", "grp")
    in_specs = (
        tile,
        P("gx", "gy"),
        P("gx", "gy"),
        tile,
        tile,
        P(),
        P(),
        P("grp", None),
        P("grp", None),
        P(None, "grp"),
        P(None, "grp"),
    )
    return jax.shard_map(body, mesh=mesh, in_specs=in_specs, out_specs=(tile,) * 5, check_vma=False)
```
